512 devices in a mesh: band: 8 (over y), gy: 8 (over z), gz: 8 (over x, core).
Axes of the slice: x: 4, y: 8, z: 8, core: 2. Of those that a mesh axis runs over, the one named last changes fastest.
Arguments:
- orbitals: float32 [1024, 48, 3840], P('band', 'gy', 'gz'), may hold values from -6 to 6
- occupied: bfloat16 [1024, 48, 3840], P('band', 'gy', 'gz'), may hold values from -6 to 6
- eigen: float32 [1024], P('band'), may hold values from -1.5 to 0
- potential: float32 [48, 3840], P('gy', 'gz'), may hold values from -2 to 0.5
- perturbation: float32 [48, 3840], P('gy', 'gz'), may hold values from 0.2 to 1.5
- precondition: float32 [48, 3840], P('gy', 'gz'), may hold values from 0.05 to 0.3
Outputs:
- updated: float32 [1024, 48, 3840], P('band', 'gy', 'gz')
- resid_norm: float32 [1024], P('band')
The draws below stay inside these ranges and needn't reach their ends.
All inputs are finite; a program needn't handle non-finite values.
Results may differ from the reference program's by a relative error of at most 0.0008.
Values may be sent and summed in bfloat16 or wider, within the bound.
A program may use at most 128 MiB of HBM per device.

```python
import math
import jax
import jax.numpy as jnp
from jax import lax

NX = 80
BANDS = 1024
NY = 48
NZ = 48


def steps_of(own_key, extent, pieces, least, high):
    gain, own = 1.0, jax.random.fold_in(own_key, 6)
    for axis_at, blocks in pieces:
        steps = jnp.exp(jax.random.uniform(jax.random.fold_in(own, axis_at), (blocks,), jnp.float32, least / len(pieces), high / len(pieces)))
        gain = gain * jnp.repeat(steps, extent[axis_at] // blocks).reshape([-1 if axis == axis_at else 1 for axis in range(len(extent))])
    return gain


def normal_values(key, dims, spread, reach, split=(), held_as=jnp.bfloat16):
    factor_of = steps_of(key, dims, split, -0.22, 0.18) if split else 1.0
    array = jax.random.normal(key, dims, jnp.float32) * spread * factor_of
    return jnp.minimum(jnp.maximum(array, -reach), reach).astype(held_as)


def setup_inputs(seed: int = 0) -> dict:
    key_of = jax.random.split(jax.random.key(seed), 7)
    return {
        "orbitals": normal_values(key_of[0], (BANDS, NY, NZ * NX), 1.0, 6.0, ((0, 8), (1, 8), (2, 8)), jnp.float32),
        "occupied": normal_values(key_of[1], (BANDS, NY, NZ * NX), 1.0, 6.0, ((0, 8), (1, 8), (2, 8))),
        "eigen": jnp.clip(-1.5 + 1.5 * jax.random.uniform(key_of[2], (BANDS,), jnp.float32) ** steps_of(key_of[2], (BANDS,), ((0, 8),), -0.2, 0.2), -1.5, 0.0),
        "potential": jnp.clip(-2.0 + 2.5 * jax.random.uniform(key_of[3], (NY, NZ * NX), jnp.float32) ** steps_of(key_of[3], (NY, NZ * NX), ((0, 8), (1, 8)), -0.2, 0.2), -2.0, 0.5),
        "perturbation": jnp.clip(0.2 + 1.3 * jax.random.uniform(key_of[4], (NY, NZ * NX), jnp.float32) ** steps_of(key_of[4], (NY, NZ * NX), ((0, 8), (1, 8)), -0.2, 0.2), 0.2, 1.5),
        "precondition": jnp.clip(jnp.exp(math.log(0.3) - 1.7917595 * jax.random.uniform(key_of[5], (NY, NZ * NX), jnp.float32) ** steps_of(key_of[5], (NY, NZ * NX), ((0, 8), (1, 8)), -0.2, 0.2)), 0.05, 0.3),
    }


stencil = (-205.0 / 72.0, 8.0 / 5.0, -1.0 / 5.0, 8.0 / 315.0, -1.0 / 560.0)

def laplace(field):
    total = 3.0 * stencil[0] * field
    for dist in range(1, 5):
        for axis in range(3):
            total = total + stencil[dist] * (jnp.roll(field, dist, axis) + jnp.roll(field, -dist, axis))
    return total

def reference(orbitals, occupied, eigen, potential, perturbation, precondition):
    grid_shape = (NY, NZ, NX)
    cells = NX * NY * NZ
    pot = potential.reshape(grid_shape)
    pert = perturbation.reshape(grid_shape)
    prec = precondition.reshape(grid_shape)

    def one_band(items):
        psi, occ, energy = items
        psi = psi.reshape(grid_shape)
        occ_wide = occ.reshape(grid_shape).astype(jnp.float32)
        resid = -0.5 * laplace(psi) + (pot - energy) * psi + pert * occ_wide
        norm = jnp.sqrt(jnp.sum(resid * resid) / cells + 1e-06)
        trial = psi - prec * resid
        return (trial.reshape(NY * NZ * NX), norm)
    trial, norms = lax.map(one_band, (orbitals, occupied, eigen))
    trial_low = lax.optimization_barrier(trial.astype(jnp.bfloat16)).astype(jnp.float32)
    occ_wide = occupied.reshape(BANDS, cells).astype(jnp.float32)
    margins = jnp.dot(occ_wide, trial_low.T, preferred_element_type=jnp.float32, precision=lax.Precision.HIGHEST) / cells
    coeff = lax.optimization_barrier(margins.astype(jnp.bfloat16)).astype(jnp.float32)
    correction = jnp.dot(coeff.T, occ_wide, preferred_element_type=jnp.float32, precision=lax.Precision.HIGHEST)
    updated = (trial - correction).reshape(BANDS, NY, NZ * NX)
    return (updated, norms)
```

```python
import functools
import jax
import jax.numpy as jnp
from jax import lax
from jax.experimental import pallas as pl
from jax.experimental.pallas import tpu as pltpu
from jax.sharding import PartitionSpec as P

NX = 80
REACH = 4
MESH = pl.DeviceIdType.MESH

stencil = (-205.0 / 72.0, 8.0 / 5.0, -1.0 / 5.0, 8.0 / 315.0, -1.0 / 560.0)


def ring_plan(groups):
    far = groups // 2
    plans = []
    for order in ((0, 1, 2, 3), (2, 3, 0, 1)):
        plan = [(k, c) for k in range(1, far) for c in order]
        plan += [(far, c) for c in order[:2]]
        plans.append(plan)
    return plans


def round_plan(groups):
    far = groups // 2
    rounds = [[0, 1, groups - 1]] if far > 1 else [[0]]
    rounds += [[k, groups - k] for k in range(2, far)]
    rounds += [[far]]
    return rounds


def kernel(
    nb, ny, nz, total_cells,
    psi_hbm, occ_hbm, eig_ref, pot_ref, per_ref, pre_ref,
    out_hbm, norm_ref,
    py, pz, fields, occ, trial, low_t, part, rs, gyb, coeff, sq_z, sq_y,
    load_sem, halo_send, halo_recv, ring_send, ring_recv,
    red_send, red_recv, sq_send, sq_recv, out_sem,
):
    rows_y, flat, bands = psi_hbm.shape
    rows_z = flat // NX
    cells = rows_y * flat
    padded = occ.shape[1]
    wide = REACH * NX
    my_b = lax.axis_index("band")
    my_y = lax.axis_index("gy")
    my_z = lax.axis_index("gz")
    sends = []

    def remote(src, dst, send, recv, **where):
        copy = pltpu.make_async_remote_copy(
            src_ref=src, dst_ref=dst, send_sem=send, recv_sem=recv,
            device_id=where, device_id_type=MESH,
        )
        copy.start()
        sends.append(copy)
        return copy

    loads = [
        pltpu.make_async_copy(occ_hbm, occ.at[0, pl.ds(0, cells)], load_sem.at[0]),
        pltpu.make_async_copy(psi_hbm, py.at[pl.ds(REACH, rows_y)], load_sem.at[1]),
        pltpu.make_async_copy(psi_hbm, pz.at[:, pl.ds(wide, flat)], load_sem.at[2]),
    ]
    for load in loads:
        load.start()
    barrier = pltpu.get_barrier_semaphore()
    greeted = 0
    for axis, me, count, steps in (
        ("band", my_b, nb, (1, nb - 1)),
        ("gy", my_y, ny, range(1, ny)),
        ("gz", my_z, nz, range(1, nz)),
    ):
        for step in steps:
            pl.semaphore_signal(
                barrier, inc=1, device_id={axis: lax.rem(me + step, count)}, device_id_type=MESH
            )
            greeted += 1
    pl.semaphore_wait(barrier, greeted)

    plans = ring_plan(nb)
    toward = (lax.rem(my_b + 1, nb), lax.rem(my_b + nb - 1, nb))
    quarter = cells // 4
    ring = [[], []]

    def slot(way, k):
        return k if way == 0 else nb - k

    def ring_start(way, entry):
        k, c = plans[way][entry]
        span = pl.ds(c * quarter, quarter)
        src = occ_hbm.at[span] if k == 1 else occ.at[slot(way, k - 1), span]
        ring[way].append(
            remote(
                src, occ.at[slot(way, k), span],
                ring_send.at[way, entry], ring_recv.at[way, entry], band=toward[way],
            )
        )

    entries = len(plans[0])
    own = min(4, entries)
    for entry in range(own):
        for way in range(2):
            ring_start(way, entry)

    y_up, y_down = lax.rem(my_y + 1, ny), lax.rem(my_y + ny - 1, ny)
    z_up, z_down = lax.rem(my_z + 1, nz), lax.rem(my_z + nz - 1, nz)
    halos = [
        remote(psi_hbm.at[pl.ds(rows_y - REACH, REACH)], py.at[pl.ds(0, REACH)],
               halo_send.at[0], halo_recv.at[0], gy=y_up),
        remote(psi_hbm.at[pl.ds(0, REACH)], py.at[pl.ds(REACH + rows_y, REACH)],
               halo_send.at[1], halo_recv.at[1], gy=y_down),
        remote(psi_hbm.at[:, pl.ds(flat - wide, wide)], pz.at[:, pl.ds(0, wide)],
               halo_send.at[2], halo_recv.at[2], gz=z_up),
        remote(psi_hbm.at[:, pl.ds(0, wide)], pz.at[:, pl.ds(wide + flat, wide)],
               halo_send.at[3], halo_recv.at[3], gz=z_down),
    ]

    arrived = 0

    def advance(upto):
        nonlocal arrived
        while arrived < min(upto, entries):
            for way in range(2):
                ring[way][arrived].wait_recv()
                if arrived + own < entries:
                    ring_start(way, arrived + own)
            arrived += 1

    if padded > cells:
        for at in range(nb):
            occ[at, cells:, :] = jnp.zeros((padded - cells, bands), occ.dtype)
        trial[cells:, :] = jnp.zeros((padded - cells, bands), trial.dtype)
    for at, ref in enumerate((pot_ref, per_ref, pre_ref)):
        columns = jnp.transpose(ref[...])
        for y in range(rows_y):
            fields[at, y * flat : (y + 1) * flat, :] = jnp.broadcast_to(
                columns[:, y : y + 1], (flat, bands)
            )
    for load in loads:
        load.wait()

    advance(4)
    for halo in halos:
        halo.wait_recv()

    energy = eig_ref[...]

    def pencil(at, squares):
        y, z = lax.div(at, rows_z), lax.rem(at, rows_z)
        base = pl.multiple_of(z * NX, 16)
        here = pl.ds(base, NX)
        row = pl.ds(pl.multiple_of(at * NX, 16), NX)
        mid = py[y + REACH, here, :]
        total = (3.0 * stencil[0]) * mid
        for dist in range(1, REACH + 1):
            pair = pltpu.roll(mid, dist, 0) + pltpu.roll(mid, NX - dist, 0)
            pair += py[y + REACH + dist, here, :] + py[y + REACH - dist, here, :]
            pair += (
                pz[y, pl.ds(pl.multiple_of(base + (REACH + dist) * NX, 16), NX), :]
                + pz[y, pl.ds(pl.multiple_of(base + (REACH - dist) * NX, 16), NX), :]
            )
            total += stencil[dist] * pair
        resid = (
            -0.5 * total
            + (fields[0, row, :] - energy) * mid
            + fields[1, row, :] * occ[0, row, :].astype(jnp.float32)
        )
        trial[row, :] = mid - fields[2, row, :] * resid
        return squares + jnp.sum((resid * resid).reshape(NX // 8, 8, bands), axis=0)

    squares = lax.fori_loop(0, rows_y * rows_z, pencil, jnp.zeros((8, bands), jnp.float32))
    advance(5)

    def spread(src, dst_of, sems, axis, me, count):
        copies = []
        for step in range(1, count):
            peer = lax.rem(me + step, count)
            copies.append(
                remote(src(peer), dst_of(peer), red_send.at[sems + (step,)],
                       red_recv.at[sems + (step,)], **{axis: peer})
            )
        return copies

    def arrive(copies):
        for copy in copies:
            copy.wait_recv()

    last = len(round_plan(nb))
    sq_z[my_z] = squares
    sq_copies = spread(lambda p: sq_z.at[my_z], lambda p: sq_z.at[my_z], (last, 0), "gz", my_z, nz)

    for at in range(padded // 128):
        block = pl.ds(at * 128, 128)
        low_t[:, block] = jnp.transpose(trial[block, :]).astype(low_t.dtype)
    advance(6)

    rounds = round_plan(nb)
    starts = [0]
    for group in rounds:
        starts.append(starts[-1] + len(group) * bands)
    share = bands // nz

    def span_of(r):
        return pl.ds(starts[r], starts[r + 1] - starts[r])

    def margins(r):
        for i, at in enumerate(rounds[r]):
            part[:, pl.ds(starts[r] + i * bands, bands)] = jnp.dot(
                low_t[...], occ[at], preferred_element_type=jnp.float32
            )
        cols = span_of(r)
        mine = pl.ds(pl.multiple_of(my_z * share, 16), share)
        copies = spread(
            lambda p: part.at[pl.ds(pl.multiple_of(p * share, 16), share), cols],
            lambda p: rs.at[my_z, :, cols],
            (r, 0), "gz", my_z, nz,
        )
        rs[my_z, :, cols] = part[mine, cols]
        return copies

    def over_y(r, copies):
        arrive(copies)
        cols = span_of(r)
        total = rs[0, :, cols]
        for at in range(1, nz):
            total += rs[at, :, cols]
        gyb[my_y, :, cols] = total
        return spread(
            lambda p: gyb.at[my_y, :, cols], lambda p: gyb.at[my_y, :, cols],
            (r, 1), "gy", my_y, ny,
        )

    def over_z(r, copies):
        arrive(copies)
        cols = span_of(r)
        total = gyb[0, :, cols]
        for at in range(1, ny):
            total += gyb[at, :, cols]
        mine = pl.ds(pl.multiple_of(my_z * share, 16), share)
        coeff[mine, cols] = (total / total_cells).astype(coeff.dtype)
        return spread(
            lambda p: coeff.at[mine, cols], lambda p: coeff.at[mine, cols],
            (r, 2), "gz", my_z, nz,
        )

    def correct(r, copies, finish=None):
        arrive(copies)

        def rows(y, carry):
            row = pl.ds(pl.multiple_of(y * flat, 16), flat)
            total = trial[row, :]
            for i, at in enumerate(rounds[r]):
                total -= lax.dot_general(
                    occ[at, row, :], coeff[:, pl.ds(starts[r] + i * bands, bands)],
                    (((1,), (1,)), ((), ())), preferred_element_type=jnp.float32,
                )
            trial[row, :] = total
            return carry

        if finish is None:
            lax.fori_loop(0, rows_y, rows, 0)
        else:
            for y in range(rows_y):
                rows(y, 0)
                finish(y)

    outs = []

    def finish(y):
        copy = pltpu.make_async_copy(
            trial.at[pl.ds(y * flat, flat)], out_hbm.at[y], out_sem.at[y]
        )
        copy.start()
        outs.append(copy)

    before = None
    for r in range(last):
        dist = r + 1
        advance(4 * dist)
        one = margins(r)
        if r == 0:
            arrive(sq_copies)
            over = sq_z[0]
            for at in range(1, nz):
                over += sq_z[at]
            sq_y[my_y] = over
            sq_copies = spread(
                lambda p: sq_y.at[my_y], lambda p: sq_y.at[my_y], (last, 1), "gy", my_y, ny
            )
        advance(4 * dist + 1)
        if before is not None:
            three = over_z(r - 1, before)
            two = over_y(r, one)
            advance(4 * dist + 2)
            correct(r - 1, three)
        else:
            two = over_y(r, one)
        before = two
    three = over_z(last - 1, before)

    arrive(sq_copies)
    over = sq_y[0]
    for at in range(1, ny):
        over += sq_y[at]
    norm_ref[...] = jnp.sqrt(jnp.sum(over, axis=0, keepdims=True) / total_cells + 1e-06)

    correct(last - 1, three, finish)
    for copy in sends:
        copy.wait_send()
    for copy in outs:
        copy.wait()


def on_device(nb, ny, nz, orbitals, occupied, eigen, potential, perturbation, precondition):
    bands, rows_y, flat = orbitals.shape
    cells = rows_y * flat
    padded = -(-cells // 128) * 128
    total_cells = float(cells * ny * nz)
    psi = jnp.transpose(orbitals, (1, 2, 0))
    occ = jnp.transpose(occupied, (1, 2, 0)).reshape(cells, bands)
    rounds = len(round_plan(nb))
    entries = len(ring_plan(nb)[0])
    share = bands // nz
    everywhere = pl.BlockSpec(memory_space=pl.ANY)
    local = pl.BlockSpec(memory_space=pltpu.VMEM)
    f32, bf16 = jnp.float32, jnp.bfloat16
    dma = pltpu.SemaphoreType.DMA
    updated, norms = pl.pallas_call(
        functools.partial(kernel, nb, ny, nz, total_cells),
        out_shape=(
            jax.ShapeDtypeStruct((rows_y, flat, bands), f32),
            jax.ShapeDtypeStruct((1, bands), f32),
        ),
        in_specs=[everywhere, everywhere, local, local, local, local],
        out_specs=(everywhere, local),
        scratch_shapes=[
            pltpu.VMEM((rows_y + 2 * REACH, flat, bands), f32),
            pltpu.VMEM((rows_y, flat + 2 * REACH * NX, bands), f32),
            pltpu.VMEM((3, cells, bands), f32),
            pltpu.VMEM((nb, padded, bands), bf16),
            pltpu.VMEM((padded, bands), f32),
            pltpu.VMEM((bands, padded), bf16),
            pltpu.VMEM((bands, nb * bands), f32),
            pltpu.VMEM((nz, share, nb * bands), f32),
            pltpu.VMEM((ny, share, nb * bands), f32),
            pltpu.VMEM((bands, nb * bands), bf16),
            pltpu.VMEM((nz, 8, bands), f32),
            pltpu.VMEM((ny, 8, bands), f32),
            dma((3,)), dma((4,)), dma((4,)), dma((2, entries)), dma((2, entries)),
            dma((rounds + 1, 3, max(ny, nz))), dma((rounds + 1, 3, max(ny, nz))),
            dma((1,)), dma((1,)), dma((rows_y,)),
        ],
        compiler_params=pltpu.CompilerParams(
            collective_id=0, has_side_effects=True, vmem_limit_bytes=60 * 1024 * 1024
        ),
        name="sternheimer",
    )(psi, occ, eigen.reshape(1, bands), potential, perturbation, precondition)
    return jnp.transpose(updated, (2, 0, 1)), norms.reshape(bands)


def solution(mesh):
    placed = (
        P("band", "gy", "gz"),
        P("band", "gy", "gz"),
        P("band"),
        P("gy", "gz"),
        P("gy", "gz"),
        P("gy", "gz"),
    )
    sizes = tuple(mesh.shape[axis] for axis in ("band", "gy", "gz"))
    return jax.shard_map(
        functools.partial(on_device, *sizes),
        mesh=mesh,
        in_specs=placed,
        out_specs=(P("band", "gy", "gz"), P("band")),
        check_vma=False,
    )
```

```python
import functools
import jax
import jax.numpy as jnp
from jax import lax
from jax.experimental import pallas as pl
from jax.experimental.pallas import tpu as pltpu
from jax.sharding import PartitionSpec as P

NX = 80
REACH = 4
MESH = pl.DeviceIdType.MESH

stencil = (-205.0 / 72.0, 8.0 / 5.0, -1.0 / 5.0, 8.0 / 315.0, -1.0 / 560.0)


def ring_plan(groups):
    far = groups // 2
    plans = []
    for order in ((0, 1, 2, 3), (2, 3, 0, 1)):
        plan = [(k, c) for k in range(1, far) for c in order]
        plan += [(far, c) for c in order[:2]]
        plans.append(plan)
    return plans


def round_plan(groups):
    far = groups // 2
    rounds = [[0, 1, groups - 1]] if far > 1 else [[0]]
    rounds += [[k, groups - k] for k in range(2, far)]
    rounds += [[far]]
    return rounds


def quarters(cells):
    return [(cells * i // 4 + 64) // 128 * 128 for i in range(4)] + [cells]


def kernel(
    nb, ny, nz, total_cells,
    psi_hbm, occ_hbm, eig_ref, pot_ref, per_ref, pre_ref,
    trial, occ_far, coeff_far, norm_ref,
    py, pz, fields, occ, low_t, part, rs, gyb, coeff, sq_z, sq_y,
    load_sem, halo_send, halo_recv, ring_send, ring_recv, red_send, red_recv,
):
    rows_y, flat, bands = psi_hbm.shape
    rows_z = flat // NX
    cells = rows_y * flat
    padded = occ.shape[1]
    wide = REACH * NX
    my_b = lax.axis_index("band")
    my_y = lax.axis_index("gy")
    my_z = lax.axis_index("gz")
    sends = []

    def remote(src, dst, send, recv, **where):
        copy = pltpu.make_async_remote_copy(
            src_ref=src, dst_ref=dst, send_sem=send, recv_sem=recv,
            device_id=where, device_id_type=MESH,
        )
        copy.start()
        sends.append(copy)
        return copy

    barrier = pltpu.get_barrier_semaphore()
    greeted = 0
    for axis, me, count, steps in (
        ("band", my_b, nb, (1, nb - 1)),
        ("gy", my_y, ny, range(1, ny)),
        ("gz", my_z, nz, range(1, nz)),
    ):
        for step in steps:
            pl.semaphore_signal(
                barrier, inc=1, device_id={axis: lax.rem(me + step, count)}, device_id_type=MESH
            )
            greeted += 1
    loads = [
        pltpu.make_async_copy(occ_hbm, occ.at[0, pl.ds(0, cells)], load_sem.at[0]),
        pltpu.make_async_copy(psi_hbm, py.at[pl.ds(REACH, rows_y)], load_sem.at[1]),
        pltpu.make_async_copy(psi_hbm, pz.at[:, pl.ds(wide, flat)], load_sem.at[2]),
    ]
    for load in loads:
        load.start()
    pl.semaphore_wait(barrier, greeted)

    plans = ring_plan(nb)
    toward = (lax.rem(my_b + 1, nb), lax.rem(my_b + nb - 1, nb))
    bounds = quarters(cells)
    far = nb // 2
    ring = [[], []]

    def shard(way, k):
        if k == far:
            return occ_far
        return occ.at[k if way == 0 else nb - k]

    def ring_start(way, entry):
        k, c = plans[way][entry]
        span = pl.ds(bounds[c], bounds[c + 1] - bounds[c])
        src = occ_hbm.at[span] if k == 1 else shard(way, k - 1).at[span]
        ring[way].append(
            remote(
                src, shard(way, k).at[span],
                ring_send.at[way, entry], ring_recv.at[way, entry], band=toward[way],
            )
        )

    entries = len(plans[0])
    own = min(4, entries)
    for entry in range(own):
        for way in range(2):
            ring_start(way, entry)

    y_up, y_down = lax.rem(my_y + 1, ny), lax.rem(my_y + ny - 1, ny)
    z_up, z_down = lax.rem(my_z + 1, nz), lax.rem(my_z + nz - 1, nz)
    halos = [
        remote(psi_hbm.at[pl.ds(rows_y - REACH, REACH)], py.at[pl.ds(0, REACH)],
               halo_send.at[0], halo_recv.at[0], gy=y_up),
        remote(psi_hbm.at[pl.ds(0, REACH)], py.at[pl.ds(REACH + rows_y, REACH)],
               halo_send.at[1], halo_recv.at[1], gy=y_down),
        remote(psi_hbm.at[:, pl.ds(flat - wide, wide)], pz.at[:, pl.ds(0, wide)],
               halo_send.at[2], halo_recv.at[2], gz=z_up),
        remote(psi_hbm.at[:, pl.ds(0, wide)], pz.at[:, pl.ds(wide + flat, wide)],
               halo_send.at[3], halo_recv.at[3], gz=z_down),
    ]

    arrived = 0

    def advance(upto):
        nonlocal arrived
        while arrived < min(upto, entries):
            for way in range(2):
                ring[way][arrived].wait_recv()
                if arrived + own < entries:
                    ring_start(way, arrived + own)
            arrived += 1

    if padded > cells:
        occ_far[cells:, :] = jnp.zeros((padded - cells, bands), occ.dtype)
        for at in range(nb):
            occ[at, cells:, :] = jnp.zeros((padded - cells, bands), occ.dtype)
        trial[cells:, :] = jnp.zeros((padded - cells, bands), trial.dtype)
    for at, ref in enumerate((pot_ref, per_ref, pre_ref)):
        columns = jnp.transpose(ref[...])
        for y in range(rows_y):
            fields[at, y * flat : (y + 1) * flat, :] = jnp.broadcast_to(
                columns[:, y : y + 1], (flat, bands)
            )
    for load in loads:
        load.wait()

    advance(4)
    for halo in halos:
        halo.wait_recv()

    energy = eig_ref[...]

    def pencil(at, squares):
        y, z = lax.div(at, rows_z), lax.rem(at, rows_z)
        base = pl.multiple_of(z * NX, 16)
        here = pl.ds(base, NX)
        row = pl.ds(pl.multiple_of(at * NX, 16), NX)
        mid = py[y + REACH, here, :]
        total = (3.0 * stencil[0]) * mid
        for dist in range(1, REACH + 1):
            pair = pltpu.roll(mid, dist, 0) + pltpu.roll(mid, NX - dist, 0)
            pair += py[y + REACH + dist, here, :] + py[y + REACH - dist, here, :]
            pair += (
                pz[y, pl.ds(pl.multiple_of(base + (REACH + dist) * NX, 16), NX), :]
                + pz[y, pl.ds(pl.multiple_of(base + (REACH - dist) * NX, 16), NX), :]
            )
            total += stencil[dist] * pair
        resid = (
            -0.5 * total
            + (fields[0, row, :] - energy) * mid
            + fields[1, row, :] * occ[0, row, :].astype(jnp.float32)
        )
        trial[row, :] = mid - fields[2, row, :] * resid
        return squares + jnp.sum((resid * resid).reshape(NX // 8, 8, bands), axis=0)

    squares = lax.fori_loop(0, rows_y * rows_z, pencil, jnp.zeros((8, bands), jnp.float32))
    advance(5)

    def spread(src, dst_of, sems, axis, me, count):
        copies = []
        for step in range(1, count):
            peer = lax.rem(me + step, count)
            copies.append(
                remote(src(peer), dst_of(peer), red_send.at[sems + (step,)],
                       red_recv.at[sems + (step,)], **{axis: peer})
            )
        return copies

    def arrive(copies):
        for copy in copies:
            copy.wait_recv()

    last = len(round_plan(nb))
    sq_z[my_z] = squares
    sq_copies = spread(lambda p: sq_z.at[my_z], lambda p: sq_z.at[my_z], (last, 0), "gz", my_z, nz)

    for at in range(padded // 128):
        block = pl.ds(at * 128, 128)
        low_t[:, block] = jnp.transpose(trial[block, :]).astype(low_t.dtype)
    advance(6)

    rounds = round_plan(nb)
    starts = [0]
    for group in rounds:
        starts.append(starts[-1] + len(group) * bands)
    share = bands // nz

    def span_of(r):
        return pl.ds(starts[r], starts[r + 1] - starts[r])

    def far_margins(chunks):
        total = 0.0
        for c in chunks:
            span = pl.ds(bounds[c], (padded if c == 3 else bounds[c + 1]) - bounds[c])
            total += jnp.dot(
                low_t[:, span], occ_far[span, :], preferred_element_type=jnp.float32
            )
        return total

    def margins(r):
        cols = span_of(r)
        if r == last - 1:
            part[:, cols] += far_margins((1, 3))
        else:
            for i, at in enumerate(rounds[r]):
                part[:, pl.ds(starts[r] + i * bands, bands)] = jnp.dot(
                    low_t[...], occ[at], preferred_element_type=jnp.float32
                )
        mine = pl.ds(pl.multiple_of(my_z * share, 16), share)
        copies = spread(
            lambda p: part.at[pl.ds(pl.multiple_of(p * share, 16), share), cols],
            lambda p: rs.at[my_z, :, cols],
            (r, 0), "gz", my_z, nz,
        )
        rs[my_z, :, cols] = part[mine, cols]
        return copies

    def over_y(r, copies):
        arrive(copies)
        cols = span_of(r)
        total = rs[0, :, cols]
        for at in range(1, nz):
            total += rs[at, :, cols]
        gyb[my_y, :, cols] = total
        return spread(
            lambda p: gyb.at[my_y, :, cols], lambda p: gyb.at[my_y, :, cols],
            (r, 1), "gy", my_y, ny,
        )

    def over_z(r, copies):
        arrive(copies)
        cols = span_of(r)
        total = gyb[0, :, cols]
        for at in range(1, ny):
            total += gyb[at, :, cols]
        mine = pl.ds(pl.multiple_of(my_z * share, 16), share)
        coeff[mine, cols] = (total / total_cells).astype(coeff.dtype)
        return spread(
            lambda p: coeff.at[mine, cols], lambda p: coeff.at[mine, cols],
            (r, 2), "gz", my_z, nz,
        )

    def correct(r, copies):
        arrive(copies)

        def rows(y, carry):
            row = pl.ds(pl.multiple_of(y * flat, 16), flat)
            total = trial[row, :]
            for i, at in enumerate(rounds[r]):
                total -= lax.dot_general(
                    occ[at, row, :], coeff[:, pl.ds(starts[r] + i * bands, bands)],
                    (((1,), (1,)), ((), ())), preferred_element_type=jnp.float32,
                )
            trial[row, :] = total
            return carry

        lax.fori_loop(0, rows_y, rows, 0)

    before = None
    for r in range(last):
        dist = r + 1
        if r == last - 1:
            advance(4 * r + 1)
            part[:, span_of(r)] = far_margins((0, 2))
        advance(4 * dist)
        one = margins(r)
        if r == 0:
            arrive(sq_copies)
            over = sq_z[0]
            for at in range(1, nz):
                over += sq_z[at]
            sq_y[my_y] = over
            sq_copies = spread(
                lambda p: sq_y.at[my_y], lambda p: sq_y.at[my_y], (last, 1), "gy", my_y, ny
            )
        advance(4 * dist + 1)
        if before is not None:
            three = over_z(r - 1, before)
            two = over_y(r, one)
            advance(4 * dist + 2)
            correct(r - 1, three)
        else:
            two = over_y(r, one)
        before = two
    three = over_z(last - 1, before)

    arrive(sq_copies)
    over = sq_y[0]
    for at in range(1, ny):
        over += sq_y[at]
    norm_ref[...] = jnp.sqrt(jnp.sum(over, axis=0, keepdims=True) / total_cells + 1e-06)

    arrive(three)
    coeff_far[...] = coeff[:, span_of(last - 1)]
    for copy in sends:
        copy.wait_send()


def far_correction(trial, occ_far, coeff_far, norm_ref, out_hbm, norm_out, held, sems):
    rows_y, flat, bands = out_hbm.shape
    norm_out[...] = norm_ref[...]
    copies = []
    for y in range(rows_y):
        row = pl.ds(y * flat, flat)
        held[row, :] = trial[row, :] - lax.dot_general(
            occ_far[row, :], coeff_far[...],
            (((1,), (1,)), ((), ())), preferred_element_type=jnp.float32,
        )
        copies.append(pltpu.make_async_copy(held.at[row], out_hbm.at[y], sems.at[y]))
        copies[-1].start()
    for copy in copies:
        copy.wait()


def on_device(nb, ny, nz, orbitals, occupied, eigen, potential, perturbation, precondition):
    bands, rows_y, flat = orbitals.shape
    cells = rows_y * flat
    padded = -(-cells // 128) * 128
    total_cells = float(cells * ny * nz)
    psi = jnp.transpose(orbitals, (1, 2, 0))
    occ = jnp.transpose(occupied, (1, 2, 0)).reshape(cells, bands)
    rounds = len(round_plan(nb))
    entries = len(ring_plan(nb)[0])
    share = bands // nz
    off_chip = pl.BlockSpec(memory_space=pltpu.HBM)
    local = pl.BlockSpec(memory_space=pltpu.VMEM)
    f32, bf16 = jnp.float32, jnp.bfloat16
    dma = pltpu.SemaphoreType.DMA
    held_bytes = padded * bands * 6 + bands * bands * 2 + 8192
    held = pl.pallas_call(
        functools.partial(kernel, nb, ny, nz, total_cells),
        out_shape=(
            pltpu.VMEM((padded, bands), f32),
            pltpu.VMEM((padded, bands), bf16),
            pltpu.VMEM((bands, bands), bf16),
            pltpu.VMEM((1, bands), f32),
        ),
        in_specs=[off_chip, off_chip, local, local, local, local],
        out_specs=(local, local, local, local),
        scratch_shapes=[
            pltpu.VMEM((rows_y + 2 * REACH, flat, bands), f32),
            pltpu.VMEM((rows_y, flat + 2 * REACH * NX, bands), f32),
            pltpu.VMEM((3, cells, bands), f32),
            pltpu.VMEM((nb, padded, bands), bf16),
            pltpu.VMEM((bands, padded), bf16),
            pltpu.VMEM((bands, nb * bands), f32),
            pltpu.VMEM((nz, share, nb * bands), f32),
            pltpu.VMEM((ny, share, nb * bands), f32),
            pltpu.VMEM((bands, nb * bands), bf16),
            pltpu.VMEM((nz, 8, bands), f32),
            pltpu.VMEM((ny, 8, bands), f32),
            dma((3,)), dma((4,)), dma((4,)), dma((2, entries)), dma((2, entries)),
            dma((rounds + 1, 3, max(ny, nz))), dma((rounds + 1, 3, max(ny, nz))),
        ],
        compiler_params=pltpu.CompilerParams(
            collective_id=0, has_side_effects=True, vmem_limit_bytes=67043328 - held_bytes
        ),
        name="sternheimer",
    )(psi, occ, eigen.reshape(1, bands), potential, perturbation, precondition)
    updated, norms = pl.pallas_call(
        far_correction,
        out_shape=(
            jax.ShapeDtypeStruct((rows_y, flat, bands), f32),
            jax.ShapeDtypeStruct((1, bands), f32),
        ),
        in_specs=[local] * 4,
        out_specs=(off_chip, local),
        scratch_shapes=[pltpu.VMEM((cells, bands), f32), dma((rows_y,))],
        compiler_params=pltpu.CompilerParams(vmem_limit_bytes=16 * 1024 * 1024),
        name="far_correction",
    )(*held)
    return jnp.transpose(updated, (2, 0, 1)), norms.reshape(bands)


def solution(mesh):
    placed = (
        P("band", "gy", "gz"),
        P("band", "gy", "gz"),
        P("band"),
        P("gy", "gz"),
        P("gy", "gz"),
        P("gy", "gz"),
    )
    sizes = tuple(mesh.shape[axis] for axis in ("band", "gy", "gz"))
    return jax.shard_map(
        functools.partial(on_device, *sizes),
        mesh=mesh,
        in_specs=placed,
        out_specs=(P("band", "gy", "gz"), P("band")),
        check_vma=False,
    )
```

```python
import functools
import jax
import jax.numpy as jnp
from jax import lax
from jax.experimental import pallas as pl
from jax.experimental.pallas import tpu as pltpu
from jax.sharding import PartitionSpec as P

NX = 80
REACH = 4
MESH = pl.DeviceIdType.MESH

stencil = (-205.0 / 72.0, 8.0 / 5.0, -1.0 / 5.0, 8.0 / 315.0, -1.0 / 560.0)


def ring_plan(groups):
    far = groups // 2
    plans = []
    for order in ((0, 1, 2, 3), (2, 3, 0, 1)):
        plan = [(k, c) for k in range(1, far) for c in order]
        plan += [(far, c) for c in order[:2]]
        plans.append(plan)
    return plans


def round_plan(groups):
    far = groups // 2
    rounds = [[0, 1, groups - 1]] if far > 1 else [[0]]
    rounds += [[k, groups - k] for k in range(2, far)]
    rounds += [[far]]
    return rounds


def quarters(cells):
    return [(cells * i // 4 + 64) // 128 * 128 for i in range(4)] + [cells]


def kernel(
    nb, ny, nz, total_cells,
    psi_hbm, occ_hbm, eig_ref, pot_ref, per_ref, pre_ref,
    trial, occ_far, coeff_far, norm_ref,
    py, pz, fields, occ, low_t, part, rs, gyb, coeff, sq_z, sq_y,
    load_sem, halo_send, halo_recv, ring_send, ring_recv, red_send, red_recv,
):
    rows_y, flat, bands = psi_hbm.shape
    rows_z = flat // NX
    cells = rows_y * flat
    padded = occ.shape[1]
    wide = REACH * NX
    my_b = lax.axis_index("band")
    my_y = lax.axis_index("gy")
    my_z = lax.axis_index("gz")
    sends = []

    def remote(src, dst, send, recv, **where):
        copy = pltpu.make_async_remote_copy(
            src_ref=src, dst_ref=dst, send_sem=send, recv_sem=recv,
            device_id=where, device_id_type=MESH,
        )
        copy.start()
        sends.append(copy)
        return copy

    barrier = pltpu.get_barrier_semaphore()
    greeted = 0
    for axis, me, count, steps in (
        ("band", my_b, nb, (1, nb - 1)),
        ("gy", my_y, ny, range(1, ny)),
        ("gz", my_z, nz, range(1, nz)),
    ):
        for step in steps:
            pl.semaphore_signal(
                barrier, inc=1, device_id={axis: lax.rem(me + step, count)}, device_id_type=MESH
            )
            greeted += 1
    loads = [
        pltpu.make_async_copy(occ_hbm, occ.at[0, pl.ds(0, cells)], load_sem.at[0]),
        pltpu.make_async_copy(psi_hbm, py.at[pl.ds(REACH, rows_y)], load_sem.at[1]),
        pltpu.make_async_copy(psi_hbm, pz.at[:, pl.ds(wide, flat)], load_sem.at[2]),
    ]
    for load in loads:
        load.start()
    pl.semaphore_wait(barrier, greeted)

    plans = ring_plan(nb)
    toward = (lax.rem(my_b + 1, nb), lax.rem(my_b + nb - 1, nb))
    bounds = quarters(cells)
    far = nb // 2
    ring = [[], []]

    def shard(way, k):
        if k == far:
            return occ_far
        return occ.at[k if way == 0 else nb - k]

    def ring_start(way, entry):
        k, c = plans[way][entry]
        span = pl.ds(bounds[c], bounds[c + 1] - bounds[c])
        src = occ_hbm.at[span] if k == 1 else shard(way, k - 1).at[span]
        ring[way].append(
            remote(
                src, shard(way, k).at[span],
                ring_send.at[way, entry], ring_recv.at[way, entry], band=toward[way],
            )
        )

    entries = len(plans[0])
    own = min(4, entries)
    for entry in range(own):
        for way in range(2):
            ring_start(way, entry)

    y_up, y_down = lax.rem(my_y + 1, ny), lax.rem(my_y + ny - 1, ny)
    z_up, z_down = lax.rem(my_z + 1, nz), lax.rem(my_z + nz - 1, nz)
    halos = [
        remote(psi_hbm.at[pl.ds(rows_y - REACH, REACH)], py.at[pl.ds(0, REACH)],
               halo_send.at[0], halo_recv.at[0], gy=y_up),
        remote(psi_hbm.at[pl.ds(0, REACH)], py.at[pl.ds(REACH + rows_y, REACH)],
               halo_send.at[1], halo_recv.at[1], gy=y_down),
        remote(psi_hbm.at[:, pl.ds(flat - wide, wide)], pz.at[:, pl.ds(0, wide)],
               halo_send.at[2], halo_recv.at[2], gz=z_up),
        remote(psi_hbm.at[:, pl.ds(0, wide)], pz.at[:, pl.ds(wide + flat, wide)],
               halo_send.at[3], halo_recv.at[3], gz=z_down),
    ]

    arrived = 0

    def advance(upto):
        nonlocal arrived
        while arrived < min(upto, entries):
            for way in range(2):
                ring[way][arrived].wait_recv()
                if arrived + own < entries:
                    ring_start(way, arrived + own)
            arrived += 1

    if padded > cells:
        occ_far[cells:, :] = jnp.zeros((padded - cells, bands), occ.dtype)
        for at in range(nb):
            occ[at, cells:, :] = jnp.zeros((padded - cells, bands), occ.dtype)
        trial[cells:, :] = jnp.zeros((padded - cells, bands), trial.dtype)
    for at, ref in enumerate((pot_ref, per_ref, pre_ref)):
        columns = jnp.transpose(ref[...])
        for y in range(rows_y):
            fields[at, y * flat : (y + 1) * flat, :] = jnp.broadcast_to(
                columns[:, y : y + 1], (flat, bands)
            )
    for load in loads:
        load.wait()

    advance(4)
    for halo in halos:
        halo.wait_recv()

    energy = eig_ref[...]

    def pencil(at, squares):
        y, z = lax.div(at, rows_z), lax.rem(at, rows_z)
        base = pl.multiple_of(z * NX, 16)
        here = pl.ds(base, NX)
        row = pl.ds(pl.multiple_of(at * NX, 16), NX)
        mid = py[y + REACH, here, :]
        total = (3.0 * stencil[0]) * mid
        for dist in range(1, REACH + 1):
            pair = pltpu.roll(mid, dist, 0) + pltpu.roll(mid, NX - dist, 0)
            pair += py[y + REACH + dist, here, :] + py[y + REACH - dist, here, :]
            pair += (
                pz[y, pl.ds(pl.multiple_of(base + (REACH + dist) * NX, 16), NX), :]
                + pz[y, pl.ds(pl.multiple_of(base + (REACH - dist) * NX, 16), NX), :]
            )
            total += stencil[dist] * pair
        resid = (
            -0.5 * total
            + (fields[0, row, :] - energy) * mid
            + fields[1, row, :] * occ[0, row, :].astype(jnp.float32)
        )
        trial[row, :] = mid - fields[2, row, :] * resid
        return squares + jnp.sum((resid * resid).reshape(NX // 8, 8, bands), axis=0)

    squares = lax.fori_loop(0, rows_y * rows_z, pencil, jnp.zeros((8, bands), jnp.float32))
    advance(5)

    def spread(src, dst_of, sems, axis, me, count):
        copies = []
        for step in range(1, count):
            peer = lax.rem(me + step, count)
            copies.append(
                remote(src(peer), dst_of(peer), red_send.at[sems + (step,)],
                       red_recv.at[sems + (step,)], **{axis: peer})
            )
        return copies

    def arrive(copies):
        for copy in copies:
            copy.wait_recv()

    last = len(round_plan(nb))
    sq_z[my_z] = squares
    sq_copies = spread(lambda p: sq_z.at[my_z], lambda p: sq_z.at[my_z], (last, 0), "gz", my_z, nz)

    for at in range(padded // 128):
        block = pl.ds(at * 128, 128)
        low_t[:, block] = jnp.transpose(trial[block, :]).astype(low_t.dtype)
    advance(6)

    rounds = round_plan(nb)
    starts = [0]
    for group in rounds:
        starts.append(starts[-1] + len(group) * bands)
    share = bands // nz

    def span_of(r):
        return pl.ds(starts[r], starts[r + 1] - starts[r])

    def far_margins(chunks):
        total = 0.0
        for c in chunks:
            span = pl.ds(bounds[c], (padded if c == 3 else bounds[c + 1]) - bounds[c])
            total += jnp.dot(
                low_t[:, span], occ_far[span, :], preferred_element_type=jnp.float32
            )
        return total

    def margins(r):
        cols = span_of(r)
        if r == last - 1:
            part[:, cols] += far_margins((1, 3))
        else:
            for i, at in enumerate(rounds[r]):
                part[:, pl.ds(starts[r] + i * bands, bands)] = jnp.dot(
                    low_t[...], occ[at], preferred_element_type=jnp.float32
                )
        mine = pl.ds(pl.multiple_of(my_z * share, 16), share)
        copies = spread(
            lambda p: part.at[pl.ds(pl.multiple_of(p * share, 16), share), cols],
            lambda p: rs.at[my_z, :, cols],
            (r, 0), "gz", my_z, nz,
        )
        rs[my_z, :, cols] = part[mine, cols]
        return copies

    def over_y(r, copies):
        arrive(copies)
        cols = span_of(r)
        total = rs[0, :, cols]
        for at in range(1, nz):
            total += rs[at, :, cols]
        gyb[my_y, :, cols] = total
        return spread(
            lambda p: gyb.at[my_y, :, cols], lambda p: gyb.at[my_y, :, cols],
            (r, 1), "gy", my_y, ny,
        )

    def over_z(r, copies):
        arrive(copies)
        cols = span_of(r)
        total = gyb[0, :, cols]
        for at in range(1, ny):
            total += gyb[at, :, cols]
        mine = pl.ds(pl.multiple_of(my_z * share, 16), share)
        rows = coeff_far.at[mine] if r == last - 1 else coeff.at[mine, cols]
        rows[...] = (total / total_cells).astype(coeff.dtype)
        return spread(lambda p: rows, lambda p: rows, (r, 2), "gz", my_z, nz)

    def correct(r, copies):
        arrive(copies)

        def rows(y, carry):
            row = pl.ds(pl.multiple_of(y * flat, 16), flat)
            total = trial[row, :]
            for i, at in enumerate(rounds[r]):
                total -= lax.dot_general(
                    occ[at, row, :], coeff[:, pl.ds(starts[r] + i * bands, bands)],
                    (((1,), (1,)), ((), ())), preferred_element_type=jnp.float32,
                )
            trial[row, :] = total
            return carry

        lax.fori_loop(0, rows_y, rows, 0)

    def settle(copies):
        for copy in copies:
            copy.wait_send()

    flying = None
    for r in range(last):
        dist, final = r + 1, r == last - 1
        if r == last - 2 and flying is not None:
            correct(flying[0], over_z(*flying))
            flying = None
        if final:
            advance(4 * r + 1)
            part[:, span_of(r)] = far_margins((0, 2))
        advance(4 * dist)
        one = margins(r)
        if r == 0:
            arrive(sq_copies)
            over = sq_z[0]
            for at in range(1, nz):
                over += sq_z[at]
            sq_y[my_y] = over
            sq_copies = spread(
                lambda p: sq_y.at[my_y], lambda p: sq_y.at[my_y], (last, 1), "gy", my_y, ny
            )
        if final and flying is not None:
            three = over_z(*flying)
        if r < last - 2:
            advance(4 * dist + 1)
        two = over_y(r, one)
        if flying is not None:
            if not final:
                three = over_z(*flying)
                advance(4 * dist + 2)
            correct(flying[0], three)
        flying = (r, two)

    arrive(sq_copies)
    over = sq_y[0]
    for at in range(1, ny):
        over += sq_y[at]
    norm_ref[...] = jnp.sqrt(jnp.sum(over, axis=0, keepdims=True) / total_cells + 1e-06)

    earlier = list(sends)
    three = over_z(*flying)
    settle(earlier)
    arrive(three)
    settle(three)


def far_correction(trial, occ_far, coeff_far, norm_ref, out_hbm, norm_out, held, sems):
    rows_y, flat, bands = out_hbm.shape
    norm_out[...] = norm_ref[...]
    copies = []
    for y in range(rows_y):
        row = pl.ds(y * flat, flat)
        held[row, :] = trial[row, :] - lax.dot_general(
            occ_far[row, :], coeff_far[...],
            (((1,), (1,)), ((), ())), preferred_element_type=jnp.float32,
        )
        copies.append(pltpu.make_async_copy(held.at[row], out_hbm.at[y], sems.at[y]))
        copies[-1].start()
    for copy in copies:
        copy.wait()


def on_device(nb, ny, nz, orbitals, occupied, eigen, potential, perturbation, precondition):
    bands, rows_y, flat = orbitals.shape
    cells = rows_y * flat
    padded = -(-cells // 128) * 128
    total_cells = float(cells * ny * nz)
    psi = jnp.transpose(orbitals, (1, 2, 0))
    occ = jnp.transpose(occupied, (1, 2, 0)).reshape(cells, bands)
    rounds = len(round_plan(nb))
    entries = len(ring_plan(nb)[0])
    share = bands // nz
    off_chip = pl.BlockSpec(memory_space=pltpu.HBM)
    local = pl.BlockSpec(memory_space=pltpu.VMEM)
    f32, bf16 = jnp.float32, jnp.bfloat16
    dma = pltpu.SemaphoreType.DMA
    held_bytes = padded * bands * 6 + bands * bands * 2 + 8192
    held = pl.pallas_call(
        functools.partial(kernel, nb, ny, nz, total_cells),
        out_shape=(
            pltpu.VMEM((padded, bands), f32),
            pltpu.VMEM((padded, bands), bf16),
            pltpu.VMEM((bands, bands), bf16),
            pltpu.VMEM((1, bands), f32),
        ),
        in_specs=[off_chip, off_chip, local, local, local, local],
        out_specs=(local, local, local, local),
        scratch_shapes=[
            pltpu.VMEM((rows_y + 2 * REACH, flat, bands), f32),
            pltpu.VMEM((rows_y, flat + 2 * REACH * NX, bands), f32),
            pltpu.VMEM((3, cells, bands), f32),
            pltpu.VMEM((nb, padded, bands), bf16),
            pltpu.VMEM((bands, padded), bf16),
            pltpu.VMEM((bands, nb * bands), f32),
            pltpu.VMEM((nz, share, nb * bands), f32),
            pltpu.VMEM((ny, share, nb * bands), f32),
            pltpu.VMEM((bands, nb * bands), bf16),
            pltpu.VMEM((nz, 8, bands), f32),
            pltpu.VMEM((ny, 8, bands), f32),
            dma((3,)), dma((4,)), dma((4,)), dma((2, entries)), dma((2, entries)),
            dma((rounds + 1, 3, max(ny, nz))), dma((rounds + 1, 3, max(ny, nz))),
        ],
        compiler_params=pltpu.CompilerParams(
            collective_id=0, has_side_effects=True, vmem_limit_bytes=67043328 - held_bytes
        ),
        name="sternheimer",
    )(psi, occ, eigen.reshape(1, bands), potential, perturbation, precondition)
    updated, norms = pl.pallas_call(
        far_correction,
        out_shape=(
            jax.ShapeDtypeStruct((rows_y, flat, bands), f32),
            jax.ShapeDtypeStruct((1, bands), f32),
        ),
        in_specs=[local] * 4,
        out_specs=(off_chip, local),
        scratch_shapes=[pltpu.VMEM((cells, bands), f32), dma((rows_y,))],
        compiler_params=pltpu.CompilerParams(vmem_limit_bytes=16 * 1024 * 1024),
        name="far_correction",
    )(*held)
    return jnp.transpose(updated, (2, 0, 1)), norms.reshape(bands)


def solution(mesh):
    placed = (
        P("band", "gy", "gz"),
        P("band", "gy", "gz"),
        P("band"),
        P("gy", "gz"),
        P("gy", "gz"),
        P("gy", "gz"),
    )
    sizes = tuple(mesh.shape[axis] for axis in ("band", "gy", "gz"))
    return jax.shard_map(
        functools.partial(on_device, *sizes),
        mesh=mesh,
        in_specs=placed,
        out_specs=(P("band", "gy", "gz"), P("band")),
        check_vma=False,
    )
```

```python
import functools
import jax
import jax.numpy as jnp
from jax import lax
from jax.experimental import pallas as pl
from jax.experimental.pallas import tpu as pltpu
from jax.sharding import PartitionSpec as P

NX = 80
REACH = 4
MESH = pl.DeviceIdType.MESH

stencil = (-205.0 / 72.0, 8.0 / 5.0, -1.0 / 5.0, 8.0 / 315.0, -1.0 / 560.0)


def ring_plan(groups):
    far = groups // 2
    plans = []
    for order in ((0, 1, 2, 3), (2, 3, 0, 1)):
        plan = [(k, c) for k in range(1, far) for c in order]
        plan += [(far, c) for c in order[:2]]
        plans.append(plan)
    return plans


def round_plan(groups):
    far = groups // 2
    rounds = [[0, 1, groups - 1]] if far > 1 else [[0]]
    rounds += [[k, groups - k] for k in range(2, far)]
    rounds += [[far]]
    return rounds


def quarters(cells):
    return [0, (cells // 4 + 64) // 128 * 128, cells // 2, (cells * 3 // 4 + 64) // 128 * 128, cells]


def kernel(
    nb, ny, nz, total_cells,
    psi_hbm, occ_hbm, eig_hbm, pot_hbm, per_hbm, pre_hbm,
    trial, occ_far, coeff_far, norm_ref,
    eig_ref, grids, py, pz, fields, occ, low_t, part, rs, gyb, coeff, sq_z, sq_y,
    load_sem, halo_send, halo_recv, ring_send, ring_recv, red_send, red_recv,
):
    rows_y, flat, bands = psi_hbm.shape
    rows_z = flat // NX
    cells = rows_y * flat
    padded = occ.shape[1]
    wide = REACH * NX
    my_b = lax.axis_index("band")
    my_y = lax.axis_index("gy")
    my_z = lax.axis_index("gz")
    sends = []

    def remote(src, dst, send, recv, **where):
        copy = pltpu.make_async_remote_copy(
            src_ref=src, dst_ref=dst, send_sem=send, recv_sem=recv,
            device_id=where, device_id_type=MESH,
        )
        copy.start()
        sends.append(copy)
        return copy

    barrier = pltpu.get_barrier_semaphore()
    greeted = 0
    for axis, me, count, steps in (
        ("band", my_b, nb, (1, nb - 1)),
        ("gy", my_y, ny, range(1, ny)),
        ("gz", my_z, nz, range(1, nz)),
    ):
        for step in steps:
            pl.semaphore_signal(
                barrier, inc=1, device_id={axis: lax.rem(me + step, count)}, device_id_type=MESH
            )
            greeted += 1
    loads = [
        pltpu.make_async_copy(occ_hbm, occ.at[0, pl.ds(0, cells)], load_sem.at[0]),
        pltpu.make_async_copy(psi_hbm, py.at[pl.ds(REACH, rows_y)], load_sem.at[1]),
        pltpu.make_async_copy(psi_hbm, pz.at[:, pl.ds(wide, flat)], load_sem.at[2]),
    ]
    small = [
        pltpu.make_async_copy(src, dst, load_sem.at[3 + i])
        for i, (src, dst) in enumerate(
            (
                (pot_hbm, grids.at[0]), (per_hbm, grids.at[1]), (pre_hbm, grids.at[2]),
                (eig_hbm, eig_ref),
            )
        )
    ]
    for load in loads + small:
        load.start()
    pl.semaphore_wait(barrier, greeted)

    plans = ring_plan(nb)
    toward = (lax.rem(my_b + 1, nb), lax.rem(my_b + nb - 1, nb))
    bounds = quarters(cells)
    far = nb // 2
    ring = [[], []]

    def shard(way, k):
        if k == far:
            return occ_far
        return occ.at[k if way == 0 else nb - k]

    def ring_start(way, entry):
        k, c = plans[way][entry]
        span = pl.ds(bounds[c], bounds[c + 1] - bounds[c])
        src = occ_hbm.at[span] if k == 1 else shard(way, k - 1).at[span]
        ring[way].append(
            remote(
                src, shard(way, k).at[span],
                ring_send.at[way, entry], ring_recv.at[way, entry], band=toward[way],
            )
        )

    entries = len(plans[0])
    own = min(4, entries)
    for entry in range(own):
        for way in range(2):
            ring_start(way, entry)

    y_up, y_down = lax.rem(my_y + 1, ny), lax.rem(my_y + ny - 1, ny)
    z_up, z_down = lax.rem(my_z + 1, nz), lax.rem(my_z + nz - 1, nz)
    halos = [
        remote(psi_hbm.at[pl.ds(rows_y - REACH, REACH)], py.at[pl.ds(0, REACH)],
               halo_send.at[0], halo_recv.at[0], gy=y_up),
        remote(psi_hbm.at[pl.ds(0, REACH)], py.at[pl.ds(REACH + rows_y, REACH)],
               halo_send.at[1], halo_recv.at[1], gy=y_down),
        remote(psi_hbm.at[:, pl.ds(flat - wide, wide)], pz.at[:, pl.ds(0, wide)],
               halo_send.at[2], halo_recv.at[2], gz=z_up),
        remote(psi_hbm.at[:, pl.ds(0, wide)], pz.at[:, pl.ds(wide + flat, wide)],
               halo_send.at[3], halo_recv.at[3], gz=z_down),
    ]

    arrived = 0

    def advance(upto):
        nonlocal arrived
        while arrived < min(upto, entries):
            for way in range(2):
                ring[way][arrived].wait_recv()
                if arrived + own < entries:
                    ring_start(way, arrived + own)
            arrived += 1

    if padded > cells:
        occ_far[cells:, :] = jnp.zeros((padded - cells, bands), occ.dtype)
        for at in range(nb):
            occ[at, cells:, :] = jnp.zeros((padded - cells, bands), occ.dtype)
        trial[cells:, :] = jnp.zeros((padded - cells, bands), trial.dtype)
    for load in small:
        load.wait()
    for at in range(3):
        columns = jnp.transpose(grids[at])
        for y in range(rows_y):
            fields[at, y * flat : (y + 1) * flat, :] = jnp.broadcast_to(
                columns[:, y : y + 1], (flat, bands)
            )
    for load in loads:
        load.wait()

    advance(4)
    for halo in halos:
        halo.wait_recv()

    energy = eig_ref[...]

    def pencil(at, squares):
        y, z = lax.div(at, rows_z), lax.rem(at, rows_z)
        base = pl.multiple_of(z * NX, 16)
        here = pl.ds(base, NX)
        row = pl.ds(pl.multiple_of(at * NX, 16), NX)
        mid = py[y + REACH, here, :]
        total = (3.0 * stencil[0]) * mid
        for dist in range(1, REACH + 1):
            pair = pltpu.roll(mid, dist, 0) + pltpu.roll(mid, NX - dist, 0)
            pair += py[y + REACH + dist, here, :] + py[y + REACH - dist, here, :]
            pair += (
                pz[y, pl.ds(pl.multiple_of(base + (REACH + dist) * NX, 16), NX), :]
                + pz[y, pl.ds(pl.multiple_of(base + (REACH - dist) * NX, 16), NX), :]
            )
            total += stencil[dist] * pair
        resid = (
            -0.5 * total
            + (fields[0, row, :] - energy) * mid
            + fields[1, row, :] * occ[0, row, :].astype(jnp.float32)
        )
        trial[row, :] = mid - fields[2, row, :] * resid
        return squares + jnp.sum((resid * resid).reshape(NX // 8, 8, bands), axis=0)

    squares = lax.fori_loop(0, rows_y * rows_z, pencil, jnp.zeros((8, bands), jnp.float32))
    advance(5)

    def spread(src, dst_of, sems, axis, me, count):
        copies = []
        for step in range(1, count):
            peer = lax.rem(me + step, count)
            copies.append(
                remote(src(peer), dst_of(peer), red_send.at[sems + (step,)],
                       red_recv.at[sems + (step,)], **{axis: peer})
            )
        return copies

    def arrive(copies):
        for copy in copies:
            copy.wait_recv()

    last = len(round_plan(nb))
    sq_z[my_z] = squares
    sq_copies = spread(lambda p: sq_z.at[my_z], lambda p: sq_z.at[my_z], (last, 0), "gz", my_z, nz)

    for at in range(padded // 128):
        block = pl.ds(at * 128, 128)
        low_t[:, block] = jnp.transpose(trial[block, :]).astype(low_t.dtype)
    advance(6)

    rounds = round_plan(nb)
    starts = [0]
    for group in rounds:
        starts.append(starts[-1] + len(group) * bands)
    share = bands // nz

    def span_of(r):
        return pl.ds(starts[r], starts[r + 1] - starts[r])

    tiles = [bounds[0], bounds[1], -(-bounds[2] // 128) * 128, bounds[3], padded]

    def far_margins(chunks):
        total = 0.0
        for c in chunks:
            span = pl.ds(tiles[c], tiles[c + 1] - tiles[c])
            total += jnp.dot(
                low_t[:, span], occ_far[span, :], preferred_element_type=jnp.float32
            )
        return total

    def margins(r):
        cols = span_of(r)
        if r == last - 1:
            part[:, cols] += far_margins((1, 3))
        else:
            for i, at in enumerate(rounds[r]):
                part[:, pl.ds(starts[r] + i * bands, bands)] = jnp.dot(
                    low_t[...], occ[at], preferred_element_type=jnp.float32
                )
        mine = pl.ds(pl.multiple_of(my_z * share, 16), share)
        copies = spread(
            lambda p: part.at[pl.ds(pl.multiple_of(p * share, 16), share), cols],
            lambda p: rs.at[my_z, :, cols],
            (r, 0), "gz", my_z, nz,
        )
        rs[my_z, :, cols] = part[mine, cols]
        return copies

    def over_y(r, copies):
        arrive(copies)
        cols = span_of(r)
        total = rs[0, :, cols]
        for at in range(1, nz):
            total += rs[at, :, cols]
        gyb[my_y, :, cols] = total
        return spread(
            lambda p: gyb.at[my_y, :, cols], lambda p: gyb.at[my_y, :, cols],
            (r, 1), "gy", my_y, ny,
        )

    def over_z(r, copies):
        arrive(copies)
        cols = span_of(r)
        total = gyb[0, :, cols]
        for at in range(1, ny):
            total += gyb[at, :, cols]
        mine = pl.ds(pl.multiple_of(my_z * share, 16), share)
        rows = coeff_far.at[mine] if r == last - 1 else coeff.at[mine, cols]
        rows[...] = (total / total_cells).astype(coeff.dtype)
        return spread(lambda p: rows, lambda p: rows, (r, 2), "gz", my_z, nz)

    def correct(r, copies):
        arrive(copies)

        def rows(y, carry):
            row = pl.ds(pl.multiple_of(y * flat, 16), flat)
            total = trial[row, :]
            for i, at in enumerate(rounds[r]):
                total -= lax.dot_general(
                    occ[at, row, :], coeff[:, pl.ds(starts[r] + i * bands, bands)],
                    (((1,), (1,)), ((), ())), preferred_element_type=jnp.float32,
                )
            trial[row, :] = total
            return carry

        lax.fori_loop(0, rows_y, rows, 0)

    def settle(copies):
        for copy in copies:
            copy.wait_send()

    flying = None
    for r in range(last):
        dist, final = r + 1, r == last - 1
        if r == last - 2 and flying is not None:
            correct(flying[0], over_z(*flying))
            flying = None
        if final:
            advance(4 * r + 1)
            part[:, span_of(r)] = far_margins((0, 2))
        advance(4 * dist)
        one = margins(r)
        if r == 0:
            arrive(sq_copies)
            over = sq_z[0]
            for at in range(1, nz):
                over += sq_z[at]
            sq_y[my_y] = over
            sq_copies = spread(
                lambda p: sq_y.at[my_y], lambda p: sq_y.at[my_y], (last, 1), "gy", my_y, ny
            )
        if not final:
            advance(4 * dist + 1 if r < last - 2 else 0)
        two = over_y(r, one)
        if flying is not None:
            three = over_z(*flying)
            if not final:
                advance(4 * dist + 2)
            correct(flying[0], three)
        flying = (r, two)

    arrive(sq_copies)
    over = sq_y[0]
    for at in range(1, ny):
        over += sq_y[at]
    norm_ref[...] = jnp.sqrt(jnp.sum(over, axis=0, keepdims=True) / total_cells + 1e-06)

    earlier = list(sends)
    three = over_z(*flying)
    settle(earlier)
    arrive(three)
    settle(three)


def far_correction(trial, occ_far, coeff_far, norm_ref, out_hbm, norm_out, held, sems):
    rows_y, flat, bands = out_hbm.shape
    copies = [pltpu.make_async_copy(norm_ref, norm_out, sems.at[rows_y])]
    copies[0].start()
    for y in range(rows_y):
        row = pl.ds(y * flat, flat)
        held[row, :] = trial[row, :] - lax.dot_general(
            occ_far[row, :], coeff_far[...],
            (((1,), (1,)), ((), ())), preferred_element_type=jnp.float32,
        )
        copies.append(pltpu.make_async_copy(held.at[row], out_hbm.at[y], sems.at[y]))
        copies[-1].start()
    for copy in copies:
        copy.wait()


def on_device(nb, ny, nz, orbitals, occupied, eigen, potential, perturbation, precondition):
    bands, rows_y, flat = orbitals.shape
    cells = rows_y * flat
    padded = -(-cells // 128) * 128
    total_cells = float(cells * ny * nz)
    psi = jnp.transpose(orbitals, (1, 2, 0))
    occ = jnp.transpose(occupied, (1, 2, 0)).reshape(cells, bands)
    rounds = len(round_plan(nb))
    entries = len(ring_plan(nb)[0])
    share = bands // nz
    off_chip = pl.BlockSpec(memory_space=pltpu.HBM)
    local = pl.BlockSpec(memory_space=pltpu.VMEM)
    f32, bf16 = jnp.float32, jnp.bfloat16
    dma = pltpu.SemaphoreType.DMA
    held_bytes = padded * bands * 6 + bands * bands * 2 + 8192
    held = pl.pallas_call(
        functools.partial(kernel, nb, ny, nz, total_cells),
        out_shape=(
            pltpu.VMEM((padded, bands), f32),
            pltpu.VMEM((padded, bands), bf16),
            pltpu.VMEM((bands, bands), bf16),
            pltpu.VMEM((1, bands), f32),
        ),
        in_specs=[off_chip] * 6,
        out_specs=(local, local, local, local),
        scratch_shapes=[
            pltpu.VMEM((1, bands), f32),
            pltpu.VMEM((3, rows_y, flat), f32),
            pltpu.VMEM((rows_y + 2 * REACH, flat, bands), f32),
            pltpu.VMEM((rows_y, flat + 2 * REACH * NX, bands), f32),
            pltpu.VMEM((3, cells, bands), f32),
            pltpu.VMEM((nb, padded, bands), bf16),
            pltpu.VMEM((bands, padded), bf16),
            pltpu.VMEM((bands, nb * bands), f32),
            pltpu.VMEM((nz, share, nb * bands), f32),
            pltpu.VMEM((ny, share, nb * bands), f32),
            pltpu.VMEM((bands, nb * bands), bf16),
            pltpu.VMEM((nz, 8, bands), f32),
            pltpu.VMEM((ny, 8, bands), f32),
            dma((7,)), dma((4,)), dma((4,)), dma((2, entries)), dma((2, entries)),
            dma((rounds + 1, 3, max(ny, nz))), dma((rounds + 1, 3, max(ny, nz))),
        ],
        compiler_params=pltpu.CompilerParams(
            collective_id=0, has_side_effects=True, vmem_limit_bytes=67043328 - held_bytes
        ),
        name="sternheimer",
    )(psi, occ, eigen.reshape(1, bands), potential, perturbation, precondition)
    updated, norms = pl.pallas_call(
        far_correction,
        out_shape=(
            jax.ShapeDtypeStruct((rows_y, flat, bands), f32),
            jax.ShapeDtypeStruct((1, bands), f32),
        ),
        in_specs=[local] * 4,
        out_specs=(off_chip, off_chip),
        scratch_shapes=[pltpu.VMEM((cells, bands), f32), dma((rows_y + 1,))],
        compiler_params=pltpu.CompilerParams(vmem_limit_bytes=16 * 1024 * 1024),
        name="far_correction",
    )(*held)
    return jnp.transpose(updated, (2, 0, 1)), norms.reshape(bands)


def solution(mesh):
    placed = (
        P("band", "gy", "gz"),
        P("band", "gy", "gz"),
        P("band"),
        P("gy", "gz"),
        P("gy", "gz"),
        P("gy", "gz"),
    )
    sizes = tuple(mesh.shape[axis] for axis in ("band", "gy", "gz"))
    return jax.shard_map(
        functools.partial(on_device, *sizes),
        mesh=mesh,
        in_specs=placed,
        out_specs=(P("band", "gy", "gz"), P("band")),
        check_vma=False,
    )
```

```python
import functools
import jax
import jax.numpy as jnp
from jax import lax
from jax.experimental import pallas as pl
from jax.experimental.pallas import tpu as pltpu
from jax.sharding import PartitionSpec as P

NX = 80
REACH = 4
MESH = pl.DeviceIdType.MESH

stencil = (-205.0 / 72.0, 8.0 / 5.0, -1.0 / 5.0, 8.0 / 315.0, -1.0 / 560.0)


def ring_plan(groups):
    far = groups // 2
    plans = []
    for order in ((0, 1, 2, 3), (2, 3, 0, 1)):
        plan = [(k, c) for k in range(1, far) for c in order]
        plan += [(far, c) for c in order[:2]]
        plans.append(plan)
    return plans


def round_plan(groups):
    far = groups // 2
    rounds = [[0, 1, groups - 1]] if far > 1 else [[0]]
    rounds += [[k, groups - k] for k in range(2, far)]
    rounds += [[far]]
    return rounds


def quarters(cells):
    return [0, (cells // 4 + 64) // 128 * 128, cells // 2, (cells * 3 // 4 + 64) // 128 * 128, cells]


def kernel(
    nb, ny, nz, total_cells,
    psi_hbm, occ_hbm, eig_hbm, pot_hbm, per_hbm, pre_hbm,
    trial, occ_far, coeff_far, norm_ref,
    eig_ref, grids, py, pz, fields, occ, low_t, part, rs, gyb,
    coeff, sq_z, sq_y,
    load_sem, halo_send, halo_recv, ring_send, ring_recv, red_send, red_recv,
):
    rows_y, flat, bands = psi_hbm.shape
    rows_z = flat // NX
    cells = rows_y * flat
    padded = occ.shape[1]
    wide = REACH * NX
    my_b = lax.axis_index("band")
    my_y = lax.axis_index("gy")
    my_z = lax.axis_index("gz")
    sends = []

    def remote(src, dst, send, recv, **where):
        copy = pltpu.make_async_remote_copy(
            src_ref=src, dst_ref=dst, send_sem=send, recv_sem=recv,
            device_id=where, device_id_type=MESH,
        )
        copy.start()
        sends.append(copy)
        return copy

    barrier = pltpu.get_barrier_semaphore()
    greeted = 0
    for axis, me, count, steps in (
        ("band", my_b, nb, (1, nb - 1)),
        ("gy", my_y, ny, range(1, ny)),
        ("gz", my_z, nz, range(1, nz)),
    ):
        for step in steps:
            pl.semaphore_signal(
                barrier, inc=1, device_id={axis: lax.rem(me + step, count)}, device_id_type=MESH
            )
            greeted += 1
    loads = [
        pltpu.make_async_copy(occ_hbm, occ.at[0, pl.ds(0, cells)], load_sem.at[0]),
        pltpu.make_async_copy(psi_hbm, py.at[pl.ds(REACH, rows_y)], load_sem.at[1]),
        pltpu.make_async_copy(psi_hbm, pz.at[:, pl.ds(wide, flat)], load_sem.at[2]),
    ]
    small = [
        pltpu.make_async_copy(src, dst, load_sem.at[3 + i])
        for i, (src, dst) in enumerate(
            (
                (pot_hbm, grids.at[0]), (per_hbm, grids.at[1]), (pre_hbm, grids.at[2]),
                (eig_hbm, eig_ref),
            )
        )
    ]
    for load in loads + small:
        load.start()
    pl.semaphore_wait(barrier, greeted)

    plans = ring_plan(nb)
    toward = (lax.rem(my_b + 1, nb), lax.rem(my_b + nb - 1, nb))
    bounds = quarters(cells)
    far = nb // 2
    ring = [[], []]

    def shard(way, k):
        if k == far:
            return occ_far
        return occ.at[k if way == 0 else nb - k]

    def ring_start(way, entry):
        k, c = plans[way][entry]
        span = pl.ds(bounds[c], bounds[c + 1] - bounds[c])
        src = occ_hbm.at[span] if k == 1 else shard(way, k - 1).at[span]
        ring[way].append(
            remote(
                src, shard(way, k).at[span],
                ring_send.at[way, entry], ring_recv.at[way, entry], band=toward[way],
            )
        )

    entries = len(plans[0])
    own = min(4, entries)
    for entry in range(own):
        for way in range(2):
            ring_start(way, entry)

    y_up, y_down = lax.rem(my_y + 1, ny), lax.rem(my_y + ny - 1, ny)
    z_up, z_down = lax.rem(my_z + 1, nz), lax.rem(my_z + nz - 1, nz)
    halos = [
        remote(psi_hbm.at[pl.ds(rows_y - REACH, REACH)], py.at[pl.ds(0, REACH)],
               halo_send.at[0], halo_recv.at[0], gy=y_up),
        remote(psi_hbm.at[pl.ds(0, REACH)], py.at[pl.ds(REACH + rows_y, REACH)],
               halo_send.at[1], halo_recv.at[1], gy=y_down),
        remote(psi_hbm.at[:, pl.ds(flat - wide, wide)], pz.at[:, pl.ds(0, wide)],
               halo_send.at[2], halo_recv.at[2], gz=z_up),
        remote(psi_hbm.at[:, pl.ds(0, wide)], pz.at[:, pl.ds(wide + flat, wide)],
               halo_send.at[3], halo_recv.at[3], gz=z_down),
    ]

    arrived = 0

    def advance(upto):
        nonlocal arrived
        while arrived < min(upto, entries):
            for way in range(2):
                ring[way][arrived].wait_recv()
                if arrived + own < entries:
                    ring_start(way, arrived + own)
            arrived += 1

    if padded > cells:
        occ_far[cells:, :] = jnp.zeros((padded - cells, bands), occ.dtype)
        for at in range(nb):
            occ[at, cells:, :] = jnp.zeros((padded - cells, bands), occ.dtype)
        trial[cells:, :] = jnp.zeros((padded - cells, bands), trial.dtype)
    for load in small:
        load.wait()
    for at in range(3):
        columns = jnp.transpose(grids[at])
        for y in range(rows_y):
            fields[at, y * flat : (y + 1) * flat, :] = jnp.broadcast_to(
                columns[:, y : y + 1], (flat, bands)
            )
    for load in loads:
        load.wait()

    advance(4)
    for halo in halos:
        halo.wait_recv()

    energy = eig_ref[...]

    def pencil(at, squares):
        y, z = lax.div(at, rows_z), lax.rem(at, rows_z)
        base = pl.multiple_of(z * NX, 16)
        here = pl.ds(base, NX)
        row = pl.ds(pl.multiple_of(at * NX, 16), NX)
        mid = py[y + REACH, here, :]
        total = (3.0 * stencil[0]) * mid
        for dist in range(1, REACH + 1):
            pair = pltpu.roll(mid, dist, 0) + pltpu.roll(mid, NX - dist, 0)
            pair += py[y + REACH + dist, here, :] + py[y + REACH - dist, here, :]
            pair += (
                pz[y, pl.ds(pl.multiple_of(base + (REACH + dist) * NX, 16), NX), :]
                + pz[y, pl.ds(pl.multiple_of(base + (REACH - dist) * NX, 16), NX), :]
            )
            total += stencil[dist] * pair
        resid = (
            -0.5 * total
            + (fields[0, row, :] - energy) * mid
            + fields[1, row, :] * occ[0, row, :].astype(jnp.float32)
        )
        trial[row, :] = mid - fields[2, row, :] * resid
        return squares + jnp.sum((resid * resid).reshape(NX // 8, 8, bands), axis=0)

    squares = lax.fori_loop(0, rows_y * rows_z, pencil, jnp.zeros((8, bands), jnp.float32))
    advance(5)

    def spread(src, dst_of, sems, axis, me, count):
        copies = []
        for step in range(1, count):
            peer = lax.rem(me + step, count)
            copies.append(
                remote(src(peer), dst_of(peer), red_send.at[sems + (step,)],
                       red_recv.at[sems + (step,)], **{axis: peer})
            )
        return copies

    def arrive(copies):
        for copy in copies:
            copy.wait_recv()

    last = len(round_plan(nb))
    sq_z[my_z] = squares
    sq_copies = spread(lambda p: sq_z.at[my_z], lambda p: sq_z.at[my_z], (last, 0), "gz", my_z, nz)

    for at in range(padded // 128):
        block = pl.ds(at * 128, 128)
        low_t[:, block] = jnp.transpose(trial[block, :]).astype(low_t.dtype)
    advance(6)

    rounds = round_plan(nb)
    starts = [0]
    for group in rounds:
        starts.append(starts[-1] + len(group) * bands)
    share = bands // nz

    def span_of(r):
        return pl.ds(starts[r], starts[r + 1] - starts[r])

    tiles = [bounds[0], bounds[1], -(-bounds[2] // 128) * 128, bounds[3], padded]

    def far_margins(chunks):
        total = 0.0
        for c in chunks:
            span = pl.ds(tiles[c], tiles[c + 1] - tiles[c])
            total += jnp.dot(
                low_t[:, span], occ_far[span, :], preferred_element_type=jnp.float32
            )
        return total

    def buffers(r):
        cols = span_of(r)
        return part.at[:, cols], rs.at[:, :, cols], gyb.at[:, :, cols]

    def margins(r):
        sums, slots, _ = buffers(r)
        if r == last - 1:
            sums[...] += far_margins((1, 3))
        else:
            for i, at in enumerate(rounds[r]):
                sums[:, i * bands : (i + 1) * bands] = jnp.dot(
                    low_t[...], occ[at], preferred_element_type=jnp.float32
                )
        copies = spread(
            lambda p: sums.at[pl.ds(pl.multiple_of(p * share, 16), share)],
            lambda p: slots.at[my_z],
            (r, 0), "gz", my_z, nz,
        )
        slots[my_z] = sums[pl.ds(pl.multiple_of(my_z * share, 16), share), :]
        return copies

    def summed(slots, count):
        total = slots[0]
        for at in range(1, count):
            total += slots[at]
        return total

    def over_y(r, copies):
        arrive(copies)
        _, slots, shares = buffers(r)
        shares[my_y] = summed(slots, nz)
        return spread(
            lambda p: shares.at[my_y], lambda p: shares.at[my_y], (r, 1), "gy", my_y, ny
        )

    def over_z(r, copies):
        arrive(copies)
        cols = span_of(r)
        total = summed(buffers(r)[2], ny)
        mine = pl.ds(pl.multiple_of(my_z * share, 16), share)
        rows = coeff_far.at[mine] if r == last - 1 else coeff.at[mine, cols]
        rows[...] = (total / total_cells).astype(coeff.dtype)
        return spread(lambda p: rows, lambda p: rows, (r, 2), "gz", my_z, nz)

    def correct(r, copies):
        arrive(copies)

        def rows(y, carry):
            row = pl.ds(pl.multiple_of(y * flat, 16), flat)
            total = trial[row, :]
            for i, at in enumerate(rounds[r]):
                total -= lax.dot_general(
                    occ[at, row, :], coeff[:, pl.ds(starts[r] + i * bands, bands)],
                    (((1,), (1,)), ((), ())), preferred_element_type=jnp.float32,
                )
            trial[row, :] = total
            return carry

        lax.fori_loop(0, rows_y, rows, 0)

    def settle(copies):
        for copy in copies:
            copy.wait_send()

    flying = None
    for r in range(last):
        dist, final = r + 1, r == last - 1
        ending = None
        if r == last - 2 and flying is not None:
            ending = (flying[0], over_z(*flying))
            flying = None
        if final:
            advance(4 * r + 1)
            part[:, span_of(r)] = far_margins((0, 2))
        advance(4 * dist)
        one = margins(r)
        if r == 0:
            arrive(sq_copies)
            over = sq_z[0]
            for at in range(1, nz):
                over += sq_z[at]
            sq_y[my_y] = over
            sq_copies = spread(
                lambda p: sq_y.at[my_y], lambda p: sq_y.at[my_y], (last, 1), "gy", my_y, ny
            )
        if ending is not None:
            correct(*ending)
        if r < last - 2:
            advance(4 * dist + 1)
        two = over_y(r, one)
        if flying is not None:
            ending = (flying[0], over_z(*flying))
            if not final:
                advance(4 * dist + 2)
                correct(*ending)
        flying = (r, two)

    arrive(sq_copies)
    over = sq_y[0]
    for at in range(1, ny):
        over += sq_y[at]
    norm_ref[...] = jnp.sqrt(jnp.sum(over, axis=0, keepdims=True) / total_cells + 1e-06)

    earlier = list(sends)
    three = over_z(*flying)
    if ending is not None:
        correct(*ending)
    settle(earlier)
    arrive(three)
    settle(three)


def far_correction(trial, occ_far, coeff_far, norm_ref, out_hbm, norm_out, held, sems):
    rows_y, flat, bands = out_hbm.shape
    copies = [pltpu.make_async_copy(norm_ref, norm_out, sems.at[rows_y])]
    copies[0].start()
    for y in range(rows_y):
        row = pl.ds(y * flat, flat)
        held[row, :] = trial[row, :] - lax.dot_general(
            occ_far[row, :], coeff_far[...],
            (((1,), (1,)), ((), ())), preferred_element_type=jnp.float32,
        )
        copies.append(pltpu.make_async_copy(held.at[row], out_hbm.at[y], sems.at[y]))
        copies[-1].start()
    for copy in copies:
        copy.wait()


def on_device(nb, ny, nz, orbitals, occupied, eigen, potential, perturbation, precondition):
    bands, rows_y, flat = orbitals.shape
    cells = rows_y * flat
    padded = -(-cells // 128) * 128
    total_cells = float(cells * ny * nz)
    psi = jnp.transpose(orbitals, (1, 2, 0))
    occ = jnp.transpose(occupied, (1, 2, 0)).reshape(cells, bands)
    rounds = len(round_plan(nb))
    entries = len(ring_plan(nb)[0])
    share = bands // nz
    off_chip = pl.BlockSpec(memory_space=pltpu.HBM)
    local = pl.BlockSpec(memory_space=pltpu.VMEM)
    f32, bf16 = jnp.float32, jnp.bfloat16
    dma = pltpu.SemaphoreType.DMA
    held_bytes = padded * bands * 6 + bands * bands * 2 + 8192
    held = pl.pallas_call(
        functools.partial(kernel, nb, ny, nz, total_cells),
        out_shape=(
            pltpu.VMEM((padded, bands), f32),
            pltpu.VMEM((padded, bands), bf16),
            pltpu.VMEM((bands, bands), bf16),
            pltpu.VMEM((1, bands), f32),
        ),
        in_specs=[off_chip] * 6,
        out_specs=(local, local, local, local),
        scratch_shapes=[
            pltpu.VMEM((1, bands), f32),
            pltpu.VMEM((3, rows_y, flat), f32),
            pltpu.VMEM((rows_y + 2 * REACH, flat, bands), f32),
            pltpu.VMEM((rows_y, flat + 2 * REACH * NX, bands), f32),
            pltpu.VMEM((3, cells, bands), f32),
            pltpu.VMEM((nb, padded, bands), bf16),
            pltpu.VMEM((bands, padded), bf16),
            pltpu.VMEM((bands, nb * bands), f32),
            pltpu.VMEM((nz, share, nb * bands), f32),
            pltpu.VMEM((ny, share, nb * bands), f32),
            pltpu.VMEM((bands, nb * bands), bf16),
            pltpu.VMEM((nz, 8, bands), f32),
            pltpu.VMEM((ny, 8, bands), f32),
            dma((7,)), dma((4,)), dma((4,)), dma((2, entries)), dma((2, entries)),
            dma((rounds + 1, 3, max(ny, nz))), dma((rounds + 1, 3, max(ny, nz))),
        ],
        compiler_params=pltpu.CompilerParams(
            collective_id=0, has_side_effects=True, vmem_limit_bytes=67043328 - held_bytes
        ),
        name="sternheimer",
    )(psi, occ, eigen.reshape(1, bands), potential, perturbation, precondition)
    updated, norms = pl.pallas_call(
        far_correction,
        out_shape=(
            jax.ShapeDtypeStruct((rows_y, flat, bands), f32),
            jax.ShapeDtypeStruct((1, bands), f32),
        ),
        in_specs=[local] * 4,
        out_specs=(off_chip, off_chip),
        scratch_shapes=[pltpu.VMEM((cells, bands), f32), dma((rows_y + 1,))],
        compiler_params=pltpu.CompilerParams(vmem_limit_bytes=16 * 1024 * 1024),
        name="far_correction",
    )(*held)
    return jnp.transpose(updated, (2, 0, 1)), norms.reshape(bands)


def solution(mesh):
    placed = (
        P("band", "gy", "gz"),
        P("band", "gy", "gz"),
        P("band"),
        P("gy", "gz"),
        P("gy", "gz"),
        P("gy", "gz"),
    )
    sizes = tuple(mesh.shape[axis] for axis in ("band", "gy", "gz"))
    return jax.shard_map(
        functools.partial(on_device, *sizes),
        mesh=mesh,
        in_specs=placed,
        out_specs=(P("band", "gy", "gz"), P("band")),
        check_vma=False,
    )
```

```python
import functools
import jax
import jax.numpy as jnp
from jax import lax
from jax.experimental import pallas as pl
from jax.experimental.pallas import tpu as pltpu
from jax.sharding import PartitionSpec as P

NX = 80
REACH = 4
MESH = pl.DeviceIdType.MESH

stencil = (-205.0 / 72.0, 8.0 / 5.0, -1.0 / 5.0, 8.0 / 315.0, -1.0 / 560.0)


def ring_plan(groups):
    far = groups // 2
    plans = []
    for order in ((0, 1, 2, 3), (2, 3, 0, 1)):
        plan = [(k, c) for k in range(1, far) for c in order]
        plan += [(far, c) for c in order[:2]]
        plans.append(plan)
    return plans


def round_plan(groups):
    far = groups // 2
    rounds = [[0, 1, groups - 1]] if far > 1 else [[0]]
    rounds += [[k, groups - k] for k in range(2, far)]
    rounds += [[far]]
    return rounds


def quarters(cells):
    return [0, (cells // 4 + 64) // 128 * 128, cells // 2, (cells * 3 // 4 + 64) // 128 * 128, cells]


def kernel(
    nb, ny, nz, total_cells,
    psi_hbm, occ_hbm, eig_hbm, pot_hbm, per_hbm, pre_hbm,
    trial, occ_far, coeff_far, norm_ref,
    eig_ref, grids, py, pz, fields, occ, low_t, part, rs, gyb,
    coeff, sq_z, sq_y,
    load_sem, halo_send, halo_recv, ring_send, ring_recv, red_send, red_recv, word,
):
    rows_y, flat, bands = psi_hbm.shape
    rows_z = flat // NX
    cells = rows_y * flat
    padded = occ.shape[1]
    wide = REACH * NX
    my_b = lax.axis_index("band")
    my_y = lax.axis_index("gy")
    my_z = lax.axis_index("gz")
    sends = []

    def remote(src, dst, send, recv, **where):
        copy = pltpu.make_async_remote_copy(
            src_ref=src, dst_ref=dst, send_sem=send, recv_sem=recv,
            device_id=where, device_id_type=MESH,
        )
        copy.start()
        sends.append(copy)
        return copy

    barrier = pltpu.get_barrier_semaphore()
    greeted = 0
    for axis, me, count, steps in (
        ("band", my_b, nb, (1, nb - 1)),
        ("gy", my_y, ny, (1, ny - 1)),
        ("gz", my_z, nz, (1, nz - 1)),
    ):
        for step in steps:
            pl.semaphore_signal(
                barrier, inc=1, device_id={axis: lax.rem(me + step, count)}, device_id_type=MESH
            )
            greeted += 1
    loads = [
        pltpu.make_async_copy(occ_hbm, occ.at[0, pl.ds(0, cells)], load_sem.at[0]),
        pltpu.make_async_copy(psi_hbm, py.at[pl.ds(REACH, rows_y)], load_sem.at[1]),
        pltpu.make_async_copy(psi_hbm, pz.at[:, pl.ds(wide, flat)], load_sem.at[2]),
    ]
    small = [
        pltpu.make_async_copy(src, dst, load_sem.at[3 + i])
        for i, (src, dst) in enumerate(
            (
                (pot_hbm, grids.at[0]), (per_hbm, grids.at[1]), (pre_hbm, grids.at[2]),
                (eig_hbm, eig_ref),
            )
        )
    ]
    for load in loads + small:
        load.start()
    pl.semaphore_wait(barrier, greeted)

    plans = ring_plan(nb)
    toward = (lax.rem(my_b + 1, nb), lax.rem(my_b + nb - 1, nb))
    bounds = quarters(cells)
    far = nb // 2
    ring = [[], []]

    def shard(way, k):
        if k == far:
            return occ_far
        return occ.at[k if way == 0 else nb - k]

    def ring_start(way, entry):
        k, c = plans[way][entry]
        span = pl.ds(bounds[c], bounds[c + 1] - bounds[c])
        src = occ_hbm.at[span] if k == 1 else shard(way, k - 1).at[span]
        ring[way].append(
            remote(
                src, shard(way, k).at[span],
                ring_send.at[way, entry], ring_recv.at[way, entry], band=toward[way],
            )
        )

    entries = len(plans[0])
    own = min(4, entries)
    for entry in range(own):
        for way in range(2):
            ring_start(way, entry)

    y_up, y_down = lax.rem(my_y + 1, ny), lax.rem(my_y + ny - 1, ny)
    z_up, z_down = lax.rem(my_z + 1, nz), lax.rem(my_z + nz - 1, nz)
    halos = [
        remote(psi_hbm.at[pl.ds(rows_y - REACH, REACH)], py.at[pl.ds(0, REACH)],
               halo_send.at[0], halo_recv.at[0], gy=y_up),
        remote(psi_hbm.at[pl.ds(0, REACH)], py.at[pl.ds(REACH + rows_y, REACH)],
               halo_send.at[1], halo_recv.at[1], gy=y_down),
        remote(psi_hbm.at[:, pl.ds(flat - wide, wide)], pz.at[:, pl.ds(0, wide)],
               halo_send.at[2], halo_recv.at[2], gz=z_up),
        remote(psi_hbm.at[:, pl.ds(0, wide)], pz.at[:, pl.ds(wide + flat, wide)],
               halo_send.at[3], halo_recv.at[3], gz=z_down),
    ]

    for wave in range(max(ny, nz) // 2 - 1):
        lines = [
            (axis, at, ups)
            for axis, at, ups, count in (("gy", 0, (y_up, y_down), ny), ("gz", 1, (z_up, z_down), nz))
            if wave < count // 2 - 1
        ]
        for axis, at, ups in lines:
            for way in range(2):
                pl.semaphore_signal(
                    word.at[at, wave, way], inc=1, device_id={axis: ups[way]}, device_id_type=MESH
                )
        for _, at, _ in lines:
            for way in range(2):
                pl.semaphore_wait(word.at[at, wave, way], 1)

    arrived = 0

    def advance(upto):
        nonlocal arrived
        while arrived < min(upto, entries):
            for way in range(2):
                ring[way][arrived].wait_recv()
                if arrived + own < entries:
                    ring_start(way, arrived + own)
            arrived += 1

    if padded > cells:
        occ_far[cells:, :] = jnp.zeros((padded - cells, bands), occ.dtype)
        for at in range(nb):
            occ[at, cells:, :] = jnp.zeros((padded - cells, bands), occ.dtype)
        trial[cells:, :] = jnp.zeros((padded - cells, bands), trial.dtype)
    for load in small:
        load.wait()
    for at in range(3):
        columns = jnp.transpose(grids[at])
        for y in range(rows_y):
            fields[at, y * flat : (y + 1) * flat, :] = jnp.broadcast_to(
                columns[:, y : y + 1], (flat, bands)
            )
    for load in loads:
        load.wait()

    advance(4)
    for halo in halos:
        halo.wait_recv()

    energy = eig_ref[...]

    def pencil(at, squares):
        y, z = lax.div(at, rows_z), lax.rem(at, rows_z)
        base = pl.multiple_of(z * NX, 16)
        here = pl.ds(base, NX)
        row = pl.ds(pl.multiple_of(at * NX, 16), NX)
        mid = py[y + REACH, here, :]
        total = (3.0 * stencil[0]) * mid
        for dist in range(1, REACH + 1):
            pair = pltpu.roll(mid, dist, 0) + pltpu.roll(mid, NX - dist, 0)
            pair += py[y + REACH + dist, here, :] + py[y + REACH - dist, here, :]
            pair += (
                pz[y, pl.ds(pl.multiple_of(base + (REACH + dist) * NX, 16), NX), :]
                + pz[y, pl.ds(pl.multiple_of(base + (REACH - dist) * NX, 16), NX), :]
            )
            total += stencil[dist] * pair
        resid = (
            -0.5 * total
            + (fields[0, row, :] - energy) * mid
            + fields[1, row, :] * occ[0, row, :].astype(jnp.float32)
        )
        trial[row, :] = mid - fields[2, row, :] * resid
        return squares + jnp.sum((resid * resid).reshape(NX // 8, 8, bands), axis=0)

    squares = lax.fori_loop(0, rows_y * rows_z, pencil, jnp.zeros((8, bands), jnp.float32))
    advance(5)

    def spread(src, dst_of, sems, axis, me, count):
        copies = []
        for step in range(1, count):
            peer = lax.rem(me + step, count)
            copies.append(
                remote(src(peer), dst_of(peer), red_send.at[sems + (step,)],
                       red_recv.at[sems + (step,)], **{axis: peer})
            )
        return copies

    def arrive(copies):
        for copy in copies:
            copy.wait_recv()

    last = len(round_plan(nb))
    sq_z[my_z] = squares
    sq_copies = spread(lambda p: sq_z.at[my_z], lambda p: sq_z.at[my_z], (last, 0), "gz", my_z, nz)

    for at in range(padded // 128):
        block = pl.ds(at * 128, 128)
        low_t[:, block] = jnp.transpose(trial[block, :]).astype(low_t.dtype)
    advance(6)

    rounds = round_plan(nb)
    starts = [0]
    for group in rounds:
        starts.append(starts[-1] + len(group) * bands)
    share = bands // nz

    def span_of(r):
        return pl.ds(starts[r], starts[r + 1] - starts[r])

    tiles = [bounds[0], bounds[1], -(-bounds[2] // 128) * 128, bounds[3], padded]

    def far_margins(chunks):
        total = 0.0
        for c in chunks:
            span = pl.ds(tiles[c], tiles[c + 1] - tiles[c])
            total += jnp.dot(
                low_t[:, span], occ_far[span, :], preferred_element_type=jnp.float32
            )
        return total

    def buffers(r):
        cols = span_of(r)
        return part.at[:, cols], rs.at[:, :, cols], gyb.at[:, :, cols]

    def margins(r):
        sums, slots, _ = buffers(r)
        if r == last - 1:
            sums[...] += far_margins((1, 3))
        else:
            for i, at in enumerate(rounds[r]):
                sums[:, i * bands : (i + 1) * bands] = jnp.dot(
                    low_t[...], occ[at], preferred_element_type=jnp.float32
                )
        copies = spread(
            lambda p: sums.at[pl.ds(pl.multiple_of(p * share, 16), share)],
            lambda p: slots.at[my_z],
            (r, 0), "gz", my_z, nz,
        )
        slots[my_z] = sums[pl.ds(pl.multiple_of(my_z * share, 16), share), :]
        return copies

    def summed(slots, count):
        total = slots[0]
        for at in range(1, count):
            total += slots[at]
        return total

    def over_y(r, copies):
        arrive(copies)
        _, slots, shares = buffers(r)
        shares[my_y] = summed(slots, nz)
        return spread(
            lambda p: shares.at[my_y], lambda p: shares.at[my_y], (r, 1), "gy", my_y, ny
        )

    def over_z(r, copies):
        arrive(copies)
        cols = span_of(r)
        total = summed(buffers(r)[2], ny)
        mine = pl.ds(pl.multiple_of(my_z * share, 16), share)
        rows = coeff_far.at[mine] if r == last - 1 else coeff.at[mine, cols]
        rows[...] = (total / total_cells).astype(coeff.dtype)
        return spread(lambda p: rows, lambda p: rows, (r, 2), "gz", my_z, nz)

    def correct(r, copies):
        arrive(copies)

        def rows(y, carry):
            row = pl.ds(pl.multiple_of(y * flat, 16), flat)
            total = trial[row, :]
            for i, at in enumerate(rounds[r]):
                total -= lax.dot_general(
                    occ[at, row, :], coeff[:, pl.ds(starts[r] + i * bands, bands)],
                    (((1,), (1,)), ((), ())), preferred_element_type=jnp.float32,
                )
            trial[row, :] = total
            return carry

        lax.fori_loop(0, rows_y, rows, 0)

    def settle(copies):
        for copy in copies:
            copy.wait_send()

    flying = None
    for r in range(last):
        dist, final = r + 1, r == last - 1
        ending = None
        if r == last - 2 and flying is not None:
            ending = (flying[0], over_z(*flying))
            flying = None
        if final:
            advance(4 * r + 1)
            part[:, span_of(r)] = far_margins((0, 2))
        advance(4 * dist)
        one = margins(r)
        if r == 0:
            arrive(sq_copies)
            over = sq_z[0]
            for at in range(1, nz):
                over += sq_z[at]
            sq_y[my_y] = over
            sq_copies = spread(
                lambda p: sq_y.at[my_y], lambda p: sq_y.at[my_y], (last, 1), "gy", my_y, ny
            )
        if ending is not None:
            correct(*ending)
        if r < last - 2:
            advance(4 * dist + 1)
        two = over_y(r, one)
        if flying is not None:
            ending = (flying[0], over_z(*flying))
            if not final:
                advance(4 * dist + 2)
                correct(*ending)
        flying = (r, two)

    arrive(sq_copies)
    over = sq_y[0]
    for at in range(1, ny):
        over += sq_y[at]
    norm_ref[...] = jnp.sqrt(jnp.sum(over, axis=0, keepdims=True) / total_cells + 1e-06)

    earlier = list(sends)
    three = over_z(*flying)
    if ending is not None:
        correct(*ending)
    settle(earlier)
    arrive(three)
    settle(three)


def far_correction(trial, occ_far, coeff_far, norm_ref, out_hbm, norm_out, held, sems):
    rows_y, flat, bands = out_hbm.shape
    copies = [pltpu.make_async_copy(norm_ref, norm_out, sems.at[rows_y])]
    copies[0].start()
    for y in range(rows_y):
        row = pl.ds(y * flat, flat)
        held[row, :] = trial[row, :] - lax.dot_general(
            occ_far[row, :], coeff_far[...],
            (((1,), (1,)), ((), ())), preferred_element_type=jnp.float32,
        )
        copies.append(pltpu.make_async_copy(held.at[row], out_hbm.at[y], sems.at[y]))
        copies[-1].start()
    for copy in copies:
        copy.wait()


def on_device(nb, ny, nz, orbitals, occupied, eigen, potential, perturbation, precondition):
    bands, rows_y, flat = orbitals.shape
    cells = rows_y * flat
    padded = -(-cells // 128) * 128
    total_cells = float(cells * ny * nz)
    psi = jnp.transpose(orbitals, (1, 2, 0))
    occ = jnp.transpose(occupied, (1, 2, 0)).reshape(cells, bands)
    rounds = len(round_plan(nb))
    entries = len(ring_plan(nb)[0])
    share = bands // nz
    off_chip = pl.BlockSpec(memory_space=pltpu.HBM)
    local = pl.BlockSpec(memory_space=pltpu.VMEM)
    f32, bf16 = jnp.float32, jnp.bfloat16
    dma = pltpu.SemaphoreType.DMA
    held_bytes = padded * bands * 6 + bands * bands * 2 + 8192
    held = pl.pallas_call(
        functools.partial(kernel, nb, ny, nz, total_cells),
        out_shape=(
            pltpu.VMEM((padded, bands), f32),
            pltpu.VMEM((padded, bands), bf16),
            pltpu.VMEM((bands, bands), bf16),
            pltpu.VMEM((1, bands), f32),
        ),
        in_specs=[off_chip] * 6,
        out_specs=(local, local, local, local),
        scratch_shapes=[
            pltpu.VMEM((1, bands), f32),
            pltpu.VMEM((3, rows_y, flat), f32),
            pltpu.VMEM((rows_y + 2 * REACH, flat, bands), f32),
            pltpu.VMEM((rows_y, flat + 2 * REACH * NX, bands), f32),
            pltpu.VMEM((3, cells, bands), f32),
            pltpu.VMEM((nb, padded, bands), bf16),
            pltpu.VMEM((bands, padded), bf16),
            pltpu.VMEM((bands, nb * bands), f32),
            pltpu.VMEM((nz, share, nb * bands), f32),
            pltpu.VMEM((ny, share, nb * bands), f32),
            pltpu.VMEM((bands, nb * bands), bf16),
            pltpu.VMEM((nz, 8, bands), f32),
            pltpu.VMEM((ny, 8, bands), f32),
            dma((7,)), dma((4,)), dma((4,)), dma((2, entries)), dma((2, entries)),
            dma((rounds + 1, 3, max(ny, nz))), dma((rounds + 1, 3, max(ny, nz))),
            pltpu.SemaphoreType.REGULAR((2, max(max(ny, nz) // 2 - 1, 1), 2)),
        ],
        compiler_params=pltpu.CompilerParams(
            collective_id=0, has_side_effects=True, vmem_limit_bytes=67043328 - held_bytes
        ),
        name="sternheimer",
    )(psi, occ, eigen.reshape(1, bands), potential, perturbation, precondition)
    updated, norms = pl.pallas_call(
        far_correction,
        out_shape=(
            jax.ShapeDtypeStruct((rows_y, flat, bands), f32),
            jax.ShapeDtypeStruct((1, bands), f32),
        ),
        in_specs=[local] * 4,
        out_specs=(off_chip, off_chip),
        scratch_shapes=[pltpu.VMEM((cells, bands), f32), dma((rows_y + 1,))],
        compiler_params=pltpu.CompilerParams(vmem_limit_bytes=16 * 1024 * 1024),
        name="far_correction",
    )(*held)
    return jnp.transpose(updated, (2, 0, 1)), norms.reshape(bands)


def solution(mesh):
    placed = (
        P("band", "gy", "gz"),
        P("band", "gy", "gz"),
        P("band"),
        P("gy", "gz"),
        P("gy", "gz"),
        P("gy", "gz"),
    )
    sizes = tuple(mesh.shape[axis] for axis in ("band", "gy", "gz"))
    return jax.shard_map(
        functools.partial(on_device, *sizes),
        mesh=mesh,
        in_specs=placed,
        out_specs=(P("band", "gy", "gz"), P("band")),
        check_vma=False,
    )
```

```python
import functools
import jax
import jax.numpy as jnp
from jax import lax
from jax.experimental import pallas as pl
from jax.experimental.pallas import tpu as pltpu
from jax.sharding import PartitionSpec as P

NX = 80
REACH = 4
MESH = pl.DeviceIdType.MESH

stencil = (-205.0 / 72.0, 8.0 / 5.0, -1.0 / 5.0, 8.0 / 315.0, -1.0 / 560.0)


def ring_plan(groups):
    far = groups // 2
    plans = []
    for order in ((0, 1, 2, 3), (2, 3, 0, 1)):
        plan = [(k, c) for k in range(1, far) for c in order]
        plan += [(far, c) for c in order[:2]]
        plans.append(plan)
    return plans


def round_plan(groups):
    far = groups // 2
    rounds = [[0, 1, groups - 1]] if far > 1 else [[0]]
    rounds += [[k, groups - k] for k in range(2, far)]
    rounds += [[far]]
    return rounds


def quarters(cells):
    return [0, (cells // 4 + 64) // 128 * 128, cells // 2, (cells * 3 // 4 + 64) // 128 * 128, cells]


def kernel(
    nb, ny, nz, total_cells,
    psi_hbm, occ_hbm, eig_hbm, pot_hbm, per_hbm, pre_hbm,
    trial, occ_far, coeff_far, norm_ref,
    eig_ref, grids, py, pz, fields, occ, low_t, part, rs, gyb,
    coeff, sq_z, sq_y,
    load_sem, halo_send, halo_recv, ring_send, ring_recv, red_send, red_recv, word,
):
    rows_y, flat, bands = psi_hbm.shape
    rows_z = flat // NX
    cells = rows_y * flat
    padded = occ.shape[1]
    wide = REACH * NX
    my_b = lax.axis_index("band")
    my_y = lax.axis_index("gy")
    my_z = lax.axis_index("gz")
    sends = []

    def remote(src, dst, send, recv, **where):
        copy = pltpu.make_async_remote_copy(
            src_ref=src, dst_ref=dst, send_sem=send, recv_sem=recv,
            device_id=where, device_id_type=MESH,
        )
        copy.start()
        sends.append(copy)
        return copy

    barrier = pltpu.get_barrier_semaphore()
    greeted = 0
    for axis, me, count, steps in (
        ("band", my_b, nb, (1, nb - 1)),
        ("gy", my_y, ny, (1, ny - 1)),
        ("gz", my_z, nz, (1, nz - 1)),
    ):
        for step in steps:
            pl.semaphore_signal(
                barrier, inc=1, device_id={axis: lax.rem(me + step, count)}, device_id_type=MESH
            )
            greeted += 1
    loads = [
        pltpu.make_async_copy(occ_hbm, occ.at[0, pl.ds(0, cells)], load_sem.at[0]),
        pltpu.make_async_copy(psi_hbm, py.at[pl.ds(REACH, rows_y)], load_sem.at[1]),
        pltpu.make_async_copy(psi_hbm, pz.at[:, pl.ds(wide, flat)], load_sem.at[2]),
    ]
    small = [
        pltpu.make_async_copy(src, dst, load_sem.at[3 + i])
        for i, (src, dst) in enumerate(
            (
                (pot_hbm, grids.at[0]), (per_hbm, grids.at[1]), (pre_hbm, grids.at[2]),
                (eig_hbm, eig_ref),
            )
        )
    ]
    pl.semaphore_wait(barrier, greeted)

    plans = ring_plan(nb)
    toward = (lax.rem(my_b + 1, nb), lax.rem(my_b + nb - 1, nb))
    bounds = quarters(cells)
    far = nb // 2
    ring = [[], []]

    def shard(way, k):
        if k == far:
            return occ_far
        return occ.at[k if way == 0 else nb - k]

    def ring_start(way, entry):
        k, c = plans[way][entry]
        span = pl.ds(bounds[c], bounds[c + 1] - bounds[c])
        src = occ_hbm.at[span] if k == 1 else shard(way, k - 1).at[span]
        ring[way].append(
            remote(
                src, shard(way, k).at[span],
                ring_send.at[way, entry], ring_recv.at[way, entry], band=toward[way],
            )
        )

    entries = len(plans[0])
    own = min(4, entries)
    for entry in range(own):
        for way in range(2):
            ring_start(way, entry)

    y_up, y_down = lax.rem(my_y + 1, ny), lax.rem(my_y + ny - 1, ny)
    z_up, z_down = lax.rem(my_z + 1, nz), lax.rem(my_z + nz - 1, nz)
    halos = [
        remote(psi_hbm.at[pl.ds(rows_y - REACH, REACH)], py.at[pl.ds(0, REACH)],
               halo_send.at[0], halo_recv.at[0], gy=y_up),
        remote(psi_hbm.at[pl.ds(0, REACH)], py.at[pl.ds(REACH + rows_y, REACH)],
               halo_send.at[1], halo_recv.at[1], gy=y_down),
        remote(psi_hbm.at[:, pl.ds(flat - wide, wide)], pz.at[:, pl.ds(0, wide)],
               halo_send.at[2], halo_recv.at[2], gz=z_up),
        remote(psi_hbm.at[:, pl.ds(0, wide)], pz.at[:, pl.ds(wide + flat, wide)],
               halo_send.at[3], halo_recv.at[3], gz=z_down),
    ]

    for load in small + loads:
        load.start()

    for wave in range(max(ny, nz) // 2 - 1):
        lines = [
            (axis, at, ups)
            for axis, at, ups, count in (("gy", 0, (y_up, y_down), ny), ("gz", 1, (z_up, z_down), nz))
            if wave < count // 2 - 1
        ]
        for axis, at, ups in lines:
            for way in range(2):
                pl.semaphore_signal(
                    word.at[at, wave, way], inc=1, device_id={axis: ups[way]}, device_id_type=MESH
                )
        for _, at, _ in lines:
            for way in range(2):
                pl.semaphore_wait(word.at[at, wave, way], 1)

    arrived = 0

    def advance(upto):
        nonlocal arrived
        while arrived < min(upto, entries):
            for way in range(2):
                ring[way][arrived].wait_recv()
                if arrived + own < entries:
                    ring_start(way, arrived + own)
            arrived += 1

    if padded > cells:
        occ_far[cells:, :] = jnp.zeros((padded - cells, bands), occ.dtype)
        for at in range(nb):
            occ[at, cells:, :] = jnp.zeros((padded - cells, bands), occ.dtype)
        trial[cells:, :] = jnp.zeros((padded - cells, bands), trial.dtype)
    for load in small:
        load.wait()
    for at in range(3):
        columns = jnp.transpose(grids[at])
        for y in range(rows_y):
            fields[at, y * flat : (y + 1) * flat, :] = jnp.broadcast_to(
                columns[:, y : y + 1], (flat, bands)
            )
    for load in loads:
        load.wait()

    advance(4)
    for halo in halos:
        halo.wait_recv()

    energy = eig_ref[...]

    def pencil(at, squares):
        y, z = lax.div(at, rows_z), lax.rem(at, rows_z)
        base = pl.multiple_of(z * NX, 16)
        here = pl.ds(base, NX)
        row = pl.ds(pl.multiple_of(at * NX, 16), NX)
        mid = py[y + REACH, here, :]
        total = (3.0 * stencil[0]) * mid
        for dist in range(1, REACH + 1):
            pair = pltpu.roll(mid, dist, 0) + pltpu.roll(mid, NX - dist, 0)
            pair += py[y + REACH + dist, here, :] + py[y + REACH - dist, here, :]
            pair += (
                pz[y, pl.ds(pl.multiple_of(base + (REACH + dist) * NX, 16), NX), :]
                + pz[y, pl.ds(pl.multiple_of(base + (REACH - dist) * NX, 16), NX), :]
            )
            total += stencil[dist] * pair
        resid = (
            -0.5 * total
            + (fields[0, row, :] - energy) * mid
            + fields[1, row, :] * occ[0, row, :].astype(jnp.float32)
        )
        trial[row, :] = mid - fields[2, row, :] * resid
        return squares + jnp.sum((resid * resid).reshape(NX // 8, 8, bands), axis=0)

    squares = lax.fori_loop(0, rows_y * rows_z, pencil, jnp.zeros((8, bands), jnp.float32))
    advance(5)

    def spread(src, dst_of, sems, axis, me, count):
        copies = []
        for step in range(1, count):
            peer = lax.rem(me + step, count)
            copies.append(
                remote(src(peer), dst_of(peer), red_send.at[sems + (step,)],
                       red_recv.at[sems + (step,)], **{axis: peer})
            )
        return copies

    def arrive(copies):
        for copy in copies:
            copy.wait_recv()

    last = len(round_plan(nb))
    sq_z[my_z] = squares
    sq_copies = spread(lambda p: sq_z.at[my_z], lambda p: sq_z.at[my_z], (last + 1, 0), "gz", my_z, nz)

    for at in range(padded // 128):
        block = pl.ds(at * 128, 128)
        low_t[:, block] = jnp.transpose(trial[block, :]).astype(low_t.dtype)
    advance(6)

    rounds = round_plan(nb)
    starts = [0]
    for group in rounds:
        starts.append(starts[-1] + len(group) * bands)
    share = bands // nz

    def span_of(r):
        return pl.ds(starts[r], starts[r + 1] - starts[r])

    tiles = [bounds[0], bounds[1], -(-bounds[2] // 128) * 128, bounds[3], padded]

    def far_margins(chunks):
        total = 0.0
        for c in chunks:
            span = pl.ds(tiles[c], tiles[c + 1] - tiles[c])
            total += jnp.dot(
                low_t[:, span], occ_far[span, :], preferred_element_type=jnp.float32
            )
        return total

    def pieces(r):
        if r == last - 1:
            return ((0, share // 2), (share // 2, share // 2))
        return ((0, share),)

    def buffers(r):
        cols = span_of(r)
        return part.at[:, cols], rs.at[:, :, cols], gyb.at[:, :, cols]

    def margins(r):
        sums, slots, _ = buffers(r)
        if r == last - 1:
            sums[...] += far_margins((1, 3))
        else:
            for i, at in enumerate(rounds[r]):
                sums[:, i * bands : (i + 1) * bands] = jnp.dot(
                    low_t[...], occ[at], preferred_element_type=jnp.float32
                )
        copies = [
            spread(
                lambda p: sums.at[pl.ds(pl.multiple_of(p * share + low, count), count)],
                lambda p: slots.at[my_z, pl.ds(low, count)],
                (r + i, 0), "gz", my_z, nz,
            )
            for i, (low, count) in enumerate(pieces(r))
        ]
        slots[my_z] = sums[pl.ds(pl.multiple_of(my_z * share, 16), share), :]
        return copies

    def summed(slots, count, rows):
        total = slots[0, rows, :]
        for at in range(1, count):
            total += slots[at, rows, :]
        return total

    def over_y(r, copies):
        _, slots, shares = buffers(r)
        out = []
        for i, (low, count) in enumerate(pieces(r)):
            rows = pl.ds(low, count)
            arrive(copies[i])
            shares[my_y, rows, :] = summed(slots, nz, rows)
            out.append(
                spread(
                    lambda p: shares.at[my_y, rows], lambda p: shares.at[my_y, rows],
                    (r + i, 1), "gy", my_y, ny,
                )
            )
        return out

    def over_z(r, copies):
        cols = span_of(r)
        out = []
        for i, (low, count) in enumerate(pieces(r)):
            arrive(copies[i])
            total = summed(buffers(r)[2], ny, pl.ds(low, count))
            mine = pl.ds(pl.multiple_of(my_z * share + low, count), count)
            rows = coeff_far.at[mine] if r == last - 1 else coeff.at[mine, cols]
            rows[...] = (total / total_cells).astype(coeff.dtype)
            out += spread(lambda p: rows, lambda p: rows, (r + i, 2), "gz", my_z, nz)
        return out

    def correct(r, copies):
        arrive(copies)

        def rows(y, carry):
            row = pl.ds(pl.multiple_of(y * flat, 16), flat)
            total = trial[row, :]
            for i, at in enumerate(rounds[r]):
                total -= lax.dot_general(
                    occ[at, row, :], coeff[:, pl.ds(starts[r] + i * bands, bands)],
                    (((1,), (1,)), ((), ())), preferred_element_type=jnp.float32,
                )
            trial[row, :] = total
            return carry

        lax.fori_loop(0, rows_y, rows, 0)

    def settle(copies):
        for copy in copies:
            copy.wait_send()

    flying = None
    for r in range(last):
        dist, final = r + 1, r == last - 1
        ending = None
        if r == last - 2 and flying is not None:
            ending = (flying[0], over_z(*flying))
            flying = None
        if final:
            advance(4 * r + 1)
            part[:, span_of(r)] = far_margins((0, 2))
        advance(4 * dist)
        one = margins(r)
        if r == 0:
            arrive(sq_copies)
            over = sq_z[0]
            for at in range(1, nz):
                over += sq_z[at]
            sq_y[my_y] = over
            sq_copies = spread(
                lambda p: sq_y.at[my_y], lambda p: sq_y.at[my_y], (last + 1, 1), "gy", my_y, ny
            )
        if ending is not None:
            correct(*ending)
        if r < last - 2:
            advance(4 * dist + 1)
        two = over_y(r, one)
        if flying is not None:
            ending = (flying[0], over_z(*flying))
            if not final:
                advance(4 * dist + 2)
                correct(*ending)
        flying = (r, two)

    arrive(sq_copies)
    over = sq_y[0]
    for at in range(1, ny):
        over += sq_y[at]
    norm_ref[...] = jnp.sqrt(jnp.sum(over, axis=0, keepdims=True) / total_cells + 1e-06)

    earlier = list(sends)
    three = over_z(*flying)
    if ending is not None:
        correct(*ending)
    settle(earlier)
    arrive(three)
    settle(three)


def far_correction(trial, occ_far, coeff_far, norm_ref, out_hbm, norm_out, held, sems):
    rows_y, flat, bands = out_hbm.shape
    copies = [pltpu.make_async_copy(norm_ref, norm_out, sems.at[rows_y])]
    copies[0].start()
    for y in range(rows_y):
        row = pl.ds(y * flat, flat)
        held[row, :] = trial[row, :] - lax.dot_general(
            occ_far[row, :], coeff_far[...],
            (((1,), (1,)), ((), ())), preferred_element_type=jnp.float32,
        )
        copies.append(pltpu.make_async_copy(held.at[row], out_hbm.at[y], sems.at[y]))
        copies[-1].start()
    for copy in copies:
        copy.wait()


def on_device(nb, ny, nz, orbitals, occupied, eigen, potential, perturbation, precondition):
    bands, rows_y, flat = orbitals.shape
    cells = rows_y * flat
    padded = -(-cells // 128) * 128
    total_cells = float(cells * ny * nz)
    psi = jnp.transpose(orbitals, (1, 2, 0))
    occ = jnp.transpose(occupied, (1, 2, 0)).reshape(cells, bands)
    rounds = len(round_plan(nb))
    entries = len(ring_plan(nb)[0])
    share = bands // nz
    off_chip = pl.BlockSpec(memory_space=pltpu.HBM)
    local = pl.BlockSpec(memory_space=pltpu.VMEM)
    f32, bf16 = jnp.float32, jnp.bfloat16
    dma = pltpu.SemaphoreType.DMA
    held_bytes = padded * bands * 6 + bands * bands * 2 + 8192
    held = pl.pallas_call(
        functools.partial(kernel, nb, ny, nz, total_cells),
        out_shape=(
            pltpu.VMEM((padded, bands), f32),
            pltpu.VMEM((padded, bands), bf16),
            pltpu.VMEM((bands, bands), bf16),
            pltpu.VMEM((1, bands), f32),
        ),
        in_specs=[off_chip] * 6,
        out_specs=(local, local, local, local),
        scratch_shapes=[
            pltpu.VMEM((1, bands), f32),
            pltpu.VMEM((3, rows_y, flat), f32),
            pltpu.VMEM((rows_y + 2 * REACH, flat, bands), f32),
            pltpu.VMEM((rows_y, flat + 2 * REACH * NX, bands), f32),
            pltpu.VMEM((3, cells, bands), f32),
            pltpu.VMEM((nb, padded, bands), bf16),
            pltpu.VMEM((bands, padded), bf16),
            pltpu.VMEM((bands, nb * bands), f32),
            pltpu.VMEM((nz, share, nb * bands), f32),
            pltpu.VMEM((ny, share, nb * bands), f32),
            pltpu.VMEM((bands, nb * bands), bf16),
            pltpu.VMEM((nz, 8, bands), f32),
            pltpu.VMEM((ny, 8, bands), f32),
            dma((7,)), dma((4,)), dma((4,)), dma((2, entries)), dma((2, entries)),
            dma((rounds + 2, 3, max(ny, nz))), dma((rounds + 2, 3, max(ny, nz))),
            pltpu.SemaphoreType.REGULAR((2, max(max(ny, nz) // 2 - 1, 1), 2)),
        ],
        compiler_params=pltpu.CompilerParams(
            collective_id=0, has_side_effects=True, vmem_limit_bytes=67043328 - held_bytes
        ),
        name="sternheimer",
    )(psi, occ, eigen.reshape(1, bands), potential, perturbation, precondition)
    updated, norms = pl.pallas_call(
        far_correction,
        out_shape=(
            jax.ShapeDtypeStruct((rows_y, flat, bands), f32),
            jax.ShapeDtypeStruct((1, bands), f32),
        ),
        in_specs=[local] * 4,
        out_specs=(off_chip, off_chip),
        scratch_shapes=[pltpu.VMEM((cells, bands), f32), dma((rows_y + 1,))],
        compiler_params=pltpu.CompilerParams(vmem_limit_bytes=16 * 1024 * 1024),
        name="far_correction",
    )(*held)
    return jnp.transpose(updated, (2, 0, 1)), norms.reshape(bands)


def solution(mesh):
    placed = (
        P("band", "gy", "gz"),
        P("band", "gy", "gz"),
        P("band"),
        P("gy", "gz"),
        P("gy", "gz"),
        P("gy", "gz"),
    )
    sizes = tuple(mesh.shape[axis] for axis in ("band", "gy", "gz"))
    return jax.shard_map(
        functools.partial(on_device, *sizes),
        mesh=mesh,
        in_specs=placed,
        out_specs=(P("band", "gy", "gz"), P("band")),
        check_vma=False,
    )
```

```python
import functools
import jax
import jax.numpy as jnp
from jax import lax
from jax.experimental import pallas as pl
from jax.experimental.pallas import tpu as pltpu
from jax.sharding import PartitionSpec as P

NX = 80
REACH = 4
MESH = pl.DeviceIdType.MESH

stencil = (-205.0 / 72.0, 8.0 / 5.0, -1.0 / 5.0, 8.0 / 315.0, -1.0 / 560.0)


def ring_plan(groups):
    far = groups // 2
    plans = []
    for order in ((0, 1, 2, 3), (2, 3, 0, 1)):
        plan = [(k, c) for k in range(1, far) for c in order]
        plan += [(far, c) for c in order[:2]]
        plans.append(plan)
    return plans


def round_plan(groups):
    far = groups // 2
    rounds = [[0, 1, groups - 1]] if far > 1 else [[0]]
    rounds += [[k, groups - k] for k in range(2, far)]
    rounds += [[far]]
    return rounds


def quarters(cells):
    return [0, (cells // 4 + 64) // 128 * 128, cells // 2, (cells * 3 // 4 + 64) // 128 * 128, cells]


def kernel(
    nb, ny, nz, total_cells,
    psi_hbm, occ_hbm, eig_hbm, pot_hbm, per_hbm, pre_hbm,
    trial, occ_far, coeff_far, norm_ref,
    eig_ref, grids, py, pz, fields, occ, low_t, part, rs, gyb,
    coeff, sq_z, sq_y,
    load_sem, halo_send, halo_recv, ring_send, ring_recv, red_send, red_recv, word,
):
    rows_y, flat, bands = psi_hbm.shape
    rows_z = flat // NX
    cells = rows_y * flat
    padded = occ.shape[1]
    wide = REACH * NX
    my_b = lax.axis_index("band")
    my_y = lax.axis_index("gy")
    my_z = lax.axis_index("gz")
    sends = []

    def remote(src, dst, send, recv, **where):
        copy = pltpu.make_async_remote_copy(
            src_ref=src, dst_ref=dst, send_sem=send, recv_sem=recv,
            device_id=where, device_id_type=MESH,
        )
        copy.start()
        sends.append(copy)
        return copy

    barrier = pltpu.get_barrier_semaphore()
    greeted = 0
    for axis, me, count, steps in (
        ("band", my_b, nb, (1, nb - 1)),
        ("gy", my_y, ny, (1, ny - 1)),
        ("gz", my_z, nz, (1, nz - 1)),
    ):
        for step in steps:
            pl.semaphore_signal(
                barrier, inc=1, device_id={axis: lax.rem(me + step, count)}, device_id_type=MESH
            )
            greeted += 1
    loads = [
        pltpu.make_async_copy(occ_hbm, occ.at[0, pl.ds(0, cells)], load_sem.at[0]),
        pltpu.make_async_copy(psi_hbm, py.at[pl.ds(REACH, rows_y)], load_sem.at[1]),
        pltpu.make_async_copy(psi_hbm, pz.at[:, pl.ds(wide, flat)], load_sem.at[2]),
    ]
    small = [
        pltpu.make_async_copy(src, dst, load_sem.at[3 + i])
        for i, (src, dst) in enumerate(
            (
                (pot_hbm, grids.at[0]), (per_hbm, grids.at[1]), (pre_hbm, grids.at[2]),
                (eig_hbm, eig_ref),
            )
        )
    ]
    for load in loads + small:
        load.start()
    pl.semaphore_wait(barrier, greeted)

    plans = ring_plan(nb)
    toward = (lax.rem(my_b + 1, nb), lax.rem(my_b + nb - 1, nb))
    bounds = quarters(cells)
    far = nb // 2
    ring = [[], []]

    def shard(way, k):
        if k == far:
            return occ_far
        return occ.at[k if way == 0 else nb - k]

    def ring_start(way, entry):
        k, c = plans[way][entry]
        span = pl.ds(bounds[c], bounds[c + 1] - bounds[c])
        src = occ_hbm.at[span] if k == 1 else shard(way, k - 1).at[span]
        ring[way].append(
            remote(
                src, shard(way, k).at[span],
                ring_send.at[way, entry], ring_recv.at[way, entry], band=toward[way],
            )
        )

    entries = len(plans[0])
    own = min(4, entries)
    for entry in range(own):
        for way in range(2):
            ring_start(way, entry)

    y_up, y_down = lax.rem(my_y + 1, ny), lax.rem(my_y + ny - 1, ny)
    z_up, z_down = lax.rem(my_z + 1, nz), lax.rem(my_z + nz - 1, nz)
    halos = [
        remote(psi_hbm.at[pl.ds(rows_y - REACH, REACH)], py.at[pl.ds(0, REACH)],
               halo_send.at[0], halo_recv.at[0], gy=y_up),
        remote(psi_hbm.at[pl.ds(0, REACH)], py.at[pl.ds(REACH + rows_y, REACH)],
               halo_send.at[1], halo_recv.at[1], gy=y_down),
        remote(psi_hbm.at[:, pl.ds(flat - wide, wide)], pz.at[:, pl.ds(0, wide)],
               halo_send.at[2], halo_recv.at[2], gz=z_up),
        remote(psi_hbm.at[:, pl.ds(0, wide)], pz.at[:, pl.ds(wide + flat, wide)],
               halo_send.at[3], halo_recv.at[3], gz=z_down),
    ]

    for wave in range(max(ny, nz) // 2 - 1):
        lines = [
            (axis, at, ups)
            for axis, at, ups, count in (("gy", 0, (y_up, y_down), ny), ("gz", 1, (z_up, z_down), nz))
            if wave < count // 2 - 1
        ]
        for axis, at, ups in lines:
            for way in range(2):
                pl.semaphore_signal(
                    word.at[at, wave, way], inc=1, device_id={axis: ups[way]}, device_id_type=MESH
                )
        for _, at, _ in lines:
            for way in range(2):
                pl.semaphore_wait(word.at[at, wave, way], 1)

    arrived = 0

    def advance(upto):
        nonlocal arrived
        while arrived < min(upto, entries):
            for way in range(2):
                ring[way][arrived].wait_recv()
                if arrived + own < entries:
                    ring_start(way, arrived + own)
            arrived += 1

    if padded > cells:
        occ_far[cells:, :] = jnp.zeros((padded - cells, bands), occ.dtype)
        for at in range(nb):
            occ[at, cells:, :] = jnp.zeros((padded - cells, bands), occ.dtype)
        trial[cells:, :] = jnp.zeros((padded - cells, bands), trial.dtype)
    for load in small:
        load.wait()
    for at in range(3):
        columns = jnp.transpose(grids[at])
        for y in range(rows_y):
            fields[at, y * flat : (y + 1) * flat, :] = jnp.broadcast_to(
                columns[:, y : y + 1], (flat, bands)
            )
    for load in loads:
        load.wait()

    advance(4)
    for halo in halos:
        halo.wait_recv()

    energy = eig_ref[...]

    def pencil(at, squares):
        y, z = lax.div(at, rows_z), lax.rem(at, rows_z)
        base = pl.multiple_of(z * NX, 16)
        here = pl.ds(base, NX)
        row = pl.ds(pl.multiple_of(at * NX, 16), NX)
        mid = py[y + REACH, here, :]
        total = (3.0 * stencil[0]) * mid
        for dist in range(1, REACH + 1):
            pair = pltpu.roll(mid, dist, 0) + pltpu.roll(mid, NX - dist, 0)
            pair += py[y + REACH + dist, here, :] + py[y + REACH - dist, here, :]
            pair += (
                pz[y, pl.ds(pl.multiple_of(base + (REACH + dist) * NX, 16), NX), :]
                + pz[y, pl.ds(pl.multiple_of(base + (REACH - dist) * NX, 16), NX), :]
            )
            total += stencil[dist] * pair
        resid = (
            -0.5 * total
            + (fields[0, row, :] - energy) * mid
            + fields[1, row, :] * occ[0, row, :].astype(jnp.float32)
        )
        trial[row, :] = mid - fields[2, row, :] * resid
        return squares + jnp.sum((resid * resid).reshape(NX // 8, 8, bands), axis=0)

    squares = lax.fori_loop(0, rows_y * rows_z, pencil, jnp.zeros((8, bands), jnp.float32))
    advance(5)

    def spread(src, dst_of, sems, axis, me, count):
        copies = []
        for step in range(1, count):
            peer = lax.rem(me + step, count)
            copies.append(
                remote(src(peer), dst_of(peer), red_send.at[sems + (step,)],
                       red_recv.at[sems + (step,)], **{axis: peer})
            )
        return copies

    def arrive(copies):
        for copy in copies:
            copy.wait_recv()

    last = len(round_plan(nb))
    sq_z[my_z] = squares
    sq_copies = spread(lambda p: sq_z.at[my_z], lambda p: sq_z.at[my_z], (last, 0), "gz", my_z, nz)

    for at in range(padded // 128):
        block = pl.ds(at * 128, 128)
        low_t[:, block] = jnp.transpose(trial[block, :]).astype(low_t.dtype)
    advance(6)

    rounds = round_plan(nb)
    starts = [0]
    for group in rounds:
        starts.append(starts[-1] + len(group) * bands)
    share = bands // nz

    def span_of(r):
        return pl.ds(starts[r], starts[r + 1] - starts[r])

    tiles = [bounds[0], bounds[1], -(-bounds[2] // 128) * 128, bounds[3], padded]

    def far_margins(chunks):
        total = 0.0
        for c in chunks:
            span = pl.ds(tiles[c], tiles[c + 1] - tiles[c])
            total += jnp.dot(
                low_t[:, span], occ_far[span, :], preferred_element_type=jnp.float32
            )
        return total

    def buffers(r):
        cols = span_of(r)
        return part.at[:, cols], rs.at[:, :, cols], gyb.at[:, :, cols]

    def margins(r):
        sums, slots, _ = buffers(r)
        if r == last - 1:
            sums[...] += far_margins((1, 3))
        else:
            for i, at in enumerate(rounds[r]):
                sums[:, i * bands : (i + 1) * bands] = jnp.dot(
                    low_t[...], occ[at], preferred_element_type=jnp.float32
                )
        copies = spread(
            lambda p: sums.at[pl.ds(pl.multiple_of(p * share, 16), share)],
            lambda p: slots.at[my_z],
            (r, 0), "gz", my_z, nz,
        )
        slots[my_z] = sums[pl.ds(pl.multiple_of(my_z * share, 16), share), :]
        return copies

    def summed(slots, count):
        total = slots[0]
        for at in range(1, count):
            total += slots[at]
        return total

    def over_y(r, copies):
        arrive(copies)
        _, slots, shares = buffers(r)
        shares[my_y] = summed(slots, nz)
        return spread(
            lambda p: shares.at[my_y], lambda p: shares.at[my_y], (r, 1), "gy", my_y, ny
        )

    def over_z(r, copies):
        arrive(copies)
        cols = span_of(r)
        total = summed(buffers(r)[2], ny)
        mine = pl.ds(pl.multiple_of(my_z * share, 16), share)
        rows = coeff_far.at[mine] if r == last - 1 else coeff.at[mine, cols]
        rows[...] = (total / total_cells).astype(coeff.dtype)
        return spread(lambda p: rows, lambda p: rows, (r, 2), "gz", my_z, nz)

    def correct(r, copies):
        arrive(copies)

        def rows(y, carry):
            row = pl.ds(pl.multiple_of(y * flat, 16), flat)
            total = trial[row, :]
            for i, at in enumerate(rounds[r]):
                total -= lax.dot_general(
                    occ[at, row, :], coeff[:, pl.ds(starts[r] + i * bands, bands)],
                    (((1,), (1,)), ((), ())), preferred_element_type=jnp.float32,
                )
            trial[row, :] = total
            return carry

        lax.fori_loop(0, rows_y, rows, 0)

    def settle(copies):
        for copy in copies:
            copy.wait_send()

    flying = None
    for r in range(last):
        dist, final = r + 1, r == last - 1
        ending = None
        if r == last - 2 and flying is not None:
            ending = (flying[0], over_z(*flying))
            flying = None
        if final:
            advance(4 * r + 1)
            part[:, span_of(r)] = far_margins((0, 2))
        advance(4 * dist)
        one = margins(r)
        if r == 0:
            arrive(sq_copies)
            over = sq_z[0]
            for at in range(1, nz):
                over += sq_z[at]
            sq_y[my_y] = over
            sq_copies = spread(
                lambda p: sq_y.at[my_y], lambda p: sq_y.at[my_y], (last, 1), "gy", my_y, ny
            )
        if ending is not None:
            correct(*ending)
        if r < last - 2:
            advance(4 * dist + 1)
        two = over_y(r, one)
        if flying is not None:
            ending = (flying[0], over_z(*flying))
            if not final:
                advance(4 * dist + 2)
                correct(*ending)
        flying = (r, two)

    arrive(sq_copies)
    over = sq_y[0]
    for at in range(1, ny):
        over += sq_y[at]
    norm_ref[...] = jnp.sqrt(jnp.sum(over, axis=0, keepdims=True) / total_cells + 1e-06)

    settle(list(sends))
    three = over_z(*flying)
    if ending is not None:
        correct(*ending)
    arrive(three)
    settle(three)


def far_correction(trial, occ_far, coeff_far, norm_ref, out_hbm, norm_out, held, sems):
    rows_y, flat, bands = out_hbm.shape
    copies = [pltpu.make_async_copy(norm_ref, norm_out, sems.at[rows_y])]
    copies[0].start()
    for y in range(rows_y):
        row = pl.ds(y * flat, flat)
        held[row, :] = trial[row, :] - lax.dot_general(
            occ_far[row, :], coeff_far[...],
            (((1,), (1,)), ((), ())), preferred_element_type=jnp.float32,
        )
        copies.append(pltpu.make_async_copy(held.at[row], out_hbm.at[y], sems.at[y]))
        copies[-1].start()
    for copy in copies:
        copy.wait()


def on_device(nb, ny, nz, orbitals, occupied, eigen, potential, perturbation, precondition):
    bands, rows_y, flat = orbitals.shape
    cells = rows_y * flat
    padded = -(-cells // 128) * 128
    total_cells = float(cells * ny * nz)
    psi = jnp.transpose(orbitals, (1, 2, 0))
    occ = jnp.transpose(occupied, (1, 2, 0)).reshape(cells, bands)
    rounds = len(round_plan(nb))
    entries = len(ring_plan(nb)[0])
    share = bands // nz
    off_chip = pl.BlockSpec(memory_space=pltpu.HBM)
    local = pl.BlockSpec(memory_space=pltpu.VMEM)
    f32, bf16 = jnp.float32, jnp.bfloat16
    dma = pltpu.SemaphoreType.DMA
    held_bytes = padded * bands * 6 + bands * bands * 2 + 8192
    held = pl.pallas_call(
        functools.partial(kernel, nb, ny, nz, total_cells),
        out_shape=(
            pltpu.VMEM((padded, bands), f32),
            pltpu.VMEM((padded, bands), bf16),
            pltpu.VMEM((bands, bands), bf16),
            pltpu.VMEM((1, bands), f32),
        ),
        in_specs=[off_chip] * 6,
        out_specs=(local, local, local, local),
        scratch_shapes=[
            pltpu.VMEM((1, bands), f32),
            pltpu.VMEM((3, rows_y, flat), f32),
            pltpu.VMEM((rows_y + 2 * REACH, flat, bands), f32),
            pltpu.VMEM((rows_y, flat + 2 * REACH * NX, bands), f32),
            pltpu.VMEM((3, cells, bands), f32),
            pltpu.VMEM((nb, padded, bands), bf16),
            pltpu.VMEM((bands, padded), bf16),
            pltpu.VMEM((bands, nb * bands), f32),
            pltpu.VMEM((nz, share, nb * bands), f32),
            pltpu.VMEM((ny, share, nb * bands), f32),
            pltpu.VMEM((bands, nb * bands), bf16),
            pltpu.VMEM((nz, 8, bands), f32),
            pltpu.VMEM((ny, 8, bands), f32),
            dma((7,)), dma((4,)), dma((4,)), dma((2, entries)), dma((2, entries)),
            dma((rounds + 1, 3, max(ny, nz))), dma((rounds + 1, 3, max(ny, nz))),
            pltpu.SemaphoreType.REGULAR((2, max(max(ny, nz) // 2 - 1, 1), 2)),
        ],
        compiler_params=pltpu.CompilerParams(
            collective_id=0, has_side_effects=True, vmem_limit_bytes=67043328 - held_bytes
        ),
        name="sternheimer",
    )(psi, occ, eigen.reshape(1, bands), potential, perturbation, precondition)
    updated, norms = pl.pallas_call(
        far_correction,
        out_shape=(
            jax.ShapeDtypeStruct((rows_y, flat, bands), f32),
            jax.ShapeDtypeStruct((1, bands), f32),
        ),
        in_specs=[local] * 4,
        out_specs=(off_chip, off_chip),
        scratch_shapes=[pltpu.VMEM((cells, bands), f32), dma((rows_y + 1,))],
        compiler_params=pltpu.CompilerParams(vmem_limit_bytes=16 * 1024 * 1024),
        name="far_correction",
    )(*held)
    return jnp.transpose(updated, (2, 0, 1)), norms.reshape(bands)


def solution(mesh):
    placed = (
        P("band", "gy", "gz"),
        P("band", "gy", "gz"),
        P("band"),
        P("gy", "gz"),
        P("gy", "gz"),
        P("gy", "gz"),
    )
    sizes = tuple(mesh.shape[axis] for axis in ("band", "gy", "gz"))
    return jax.shard_map(
        functools.partial(on_device, *sizes),
        mesh=mesh,
        in_specs=placed,
        out_specs=(P("band", "gy", "gz"), P("band")),
        check_vma=False,
    )
```

```python
import functools
import jax
import jax.numpy as jnp
from jax import lax
from jax.experimental import pallas as pl
from jax.experimental.pallas import tpu as pltpu
from jax.sharding import PartitionSpec as P

NX = 80
REACH = 4
MESH = pl.DeviceIdType.MESH

stencil = (-205.0 / 72.0, 8.0 / 5.0, -1.0 / 5.0, 8.0 / 315.0, -1.0 / 560.0)


def ring_plan(groups):
    far = groups // 2
    plans = []
    for order in ((0, 1, 2, 3), (2, 3, 0, 1)):
        plan = [(k, c) for k in range(1, far) for c in order]
        plan += [(far, c) for c in order[:2]]
        plans.append(plan)
    return plans


def round_plan(groups):
    far = groups // 2
    rounds = [[0, 1, groups - 1]] if far > 1 else [[0]]
    rounds += [[k, groups - k] for k in range(2, far)]
    rounds += [[far]]
    return rounds


def quarters(cells):
    return [0, (cells // 4 + 64) // 128 * 128, cells // 2, (cells * 3 // 4 + 64) // 128 * 128, cells]


def kernel(
    nb, ny, nz, total_cells,
    psi_hbm, occ_hbm, eig_hbm, pot_hbm, per_hbm, pre_hbm,
    trial, occ_far, coeff_far, norm_ref,
    eig_ref, grids, py, pz, fields, occ, low_t, part, rs, gyb,
    coeff, sq_z, sq_y,
    load_sem, halo_send, halo_recv, ring_send, ring_recv, red_send, red_recv, word,
):
    rows_y, flat, bands = psi_hbm.shape
    rows_z = flat // NX
    cells = rows_y * flat
    padded = occ.shape[1]
    wide = REACH * NX
    my_b = lax.axis_index("band")
    my_y = lax.axis_index("gy")
    my_z = lax.axis_index("gz")
    sends = []

    def remote(src, dst, send, recv, **where):
        copy = pltpu.make_async_remote_copy(
            src_ref=src, dst_ref=dst, send_sem=send, recv_sem=recv,
            device_id=where, device_id_type=MESH,
        )
        copy.start()
        sends.append(copy)
        return copy

    barrier = pltpu.get_barrier_semaphore()
    greeted = 0
    for axis, me, count, steps in (
        ("band", my_b, nb, (1, nb - 1)),
        ("gy", my_y, ny, (1, ny - 1)),
        ("gz", my_z, nz, (1, nz - 1)),
    ):
        for step in steps:
            pl.semaphore_signal(
                barrier, inc=1, device_id={axis: lax.rem(me + step, count)}, device_id_type=MESH
            )
            greeted += 1
    loads = [
        pltpu.make_async_copy(occ_hbm, occ.at[0, pl.ds(0, cells)], load_sem.at[0]),
        pltpu.make_async_copy(psi_hbm, py.at[pl.ds(REACH, rows_y)], load_sem.at[1]),
        pltpu.make_async_copy(psi_hbm, pz.at[:, pl.ds(wide, flat)], load_sem.at[2]),
    ]
    small = [
        pltpu.make_async_copy(src, dst, load_sem.at[3 + i])
        for i, (src, dst) in enumerate(
            (
                (pot_hbm, grids.at[0]), (per_hbm, grids.at[1]), (pre_hbm, grids.at[2]),
                (eig_hbm, eig_ref),
            )
        )
    ]
    pl.semaphore_wait(barrier, greeted)

    plans = ring_plan(nb)
    toward = (lax.rem(my_b + 1, nb), lax.rem(my_b + nb - 1, nb))
    bounds = quarters(cells)
    far = nb // 2
    ring = [[], []]

    def shard(way, k):
        if k == far:
            return occ_far
        return occ.at[k if way == 0 else nb - k]

    def ring_start(way, entry):
        k, c = plans[way][entry]
        span = pl.ds(bounds[c], bounds[c + 1] - bounds[c])
        src = occ_hbm.at[span] if k == 1 else shard(way, k - 1).at[span]
        ring[way].append(
            remote(
                src, shard(way, k).at[span],
                ring_send.at[way, entry], ring_recv.at[way, entry], band=toward[way],
            )
        )

    entries = len(plans[0])
    own = min(4, entries)
    for entry in range(own):
        for way in range(2):
            ring_start(way, entry)

    y_up, y_down = lax.rem(my_y + 1, ny), lax.rem(my_y + ny - 1, ny)
    z_up, z_down = lax.rem(my_z + 1, nz), lax.rem(my_z + nz - 1, nz)
    halos = [
        remote(psi_hbm.at[pl.ds(rows_y - REACH, REACH)], py.at[pl.ds(0, REACH)],
               halo_send.at[0], halo_recv.at[0], gy=y_up),
        remote(psi_hbm.at[pl.ds(0, REACH)], py.at[pl.ds(REACH + rows_y, REACH)],
               halo_send.at[1], halo_recv.at[1], gy=y_down),
        remote(psi_hbm.at[:, pl.ds(flat - wide, wide)], pz.at[:, pl.ds(0, wide)],
               halo_send.at[2], halo_recv.at[2], gz=z_up),
        remote(psi_hbm.at[:, pl.ds(0, wide)], pz.at[:, pl.ds(wide + flat, wide)],
               halo_send.at[3], halo_recv.at[3], gz=z_down),
    ]

    for load in small + loads:
        load.start()

    for wave in range(max(ny, nz) // 2 - 1):
        lines = [
            (axis, at, ups)
            for axis, at, ups, count in (("gy", 0, (y_up, y_down), ny), ("gz", 1, (z_up, z_down), nz))
            if wave < count // 2 - 1
        ]
        for axis, at, ups in lines:
            for way in range(2):
                pl.semaphore_signal(
                    word.at[at, wave, way], inc=1, device_id={axis: ups[way]}, device_id_type=MESH
                )
        for _, at, _ in lines:
            for way in range(2):
                pl.semaphore_wait(word.at[at, wave, way], 1)

    arrived = 0

    def advance(upto):
        nonlocal arrived
        while arrived < min(upto, entries):
            for way in range(2):
                ring[way][arrived].wait_recv()
                if arrived + own < entries:
                    ring_start(way, arrived + own)
            arrived += 1

    if padded > cells:
        occ_far[cells:, :] = jnp.zeros((padded - cells, bands), occ.dtype)
        for at in range(nb):
            occ[at, cells:, :] = jnp.zeros((padded - cells, bands), occ.dtype)
        trial[cells:, :] = jnp.zeros((padded - cells, bands), trial.dtype)
    for load in small:
        load.wait()
    for at in range(3):
        columns = jnp.transpose(grids[at])
        for y in range(rows_y):
            fields[at, y * flat : (y + 1) * flat, :] = jnp.broadcast_to(
                columns[:, y : y + 1], (flat, bands)
            )
    for load in loads:
        load.wait()

    advance(4)
    for halo in halos:
        halo.wait_recv()

    energy = eig_ref[...]

    def pencil(at, squares):
        y, z = lax.div(at, rows_z), lax.rem(at, rows_z)
        base = pl.multiple_of(z * NX, 16)
        here = pl.ds(base, NX)
        row = pl.ds(pl.multiple_of(at * NX, 16), NX)
        mid = py[y + REACH, here, :]
        total = (3.0 * stencil[0]) * mid
        for dist in range(1, REACH + 1):
            pair = pltpu.roll(mid, dist, 0) + pltpu.roll(mid, NX - dist, 0)
            pair += py[y + REACH + dist, here, :] + py[y + REACH - dist, here, :]
            pair += (
                pz[y, pl.ds(pl.multiple_of(base + (REACH + dist) * NX, 16), NX), :]
                + pz[y, pl.ds(pl.multiple_of(base + (REACH - dist) * NX, 16), NX), :]
            )
            total += stencil[dist] * pair
        resid = (
            -0.5 * total
            + (fields[0, row, :] - energy) * mid
            + fields[1, row, :] * occ[0, row, :].astype(jnp.float32)
        )
        trial[row, :] = mid - fields[2, row, :] * resid
        return squares + jnp.sum((resid * resid).reshape(NX // 8, 8, bands), axis=0)

    squares = lax.fori_loop(0, rows_y * rows_z, pencil, jnp.zeros((8, bands), jnp.float32))
    advance(5)

    def spread(src, dst_of, sems, axis, me, count):
        copies = []
        for step in range(1, count):
            peer = lax.rem(me + step, count)
            copies.append(
                remote(src(peer), dst_of(peer), red_send.at[sems + (step,)],
                       red_recv.at[sems + (step,)], **{axis: peer})
            )
        return copies

    def arrive(copies):
        for copy in copies:
            copy.wait_recv()

    last = len(round_plan(nb))
    sq_z[my_z] = squares
    sq_copies = spread(lambda p: sq_z.at[my_z], lambda p: sq_z.at[my_z], (last, 0), "gz", my_z, nz)

    for at in range(padded // 128):
        block = pl.ds(at * 128, 128)
        low_t[:, block] = jnp.transpose(trial[block, :]).astype(low_t.dtype)
    advance(6)

    rounds = round_plan(nb)
    starts = [0]
    for group in rounds:
        starts.append(starts[-1] + len(group) * bands)
    share = bands // nz

    def span_of(r):
        return pl.ds(starts[r], starts[r + 1] - starts[r])

    tiles = [bounds[0], bounds[1], -(-bounds[2] // 128) * 128, bounds[3], padded]

    def far_margins(chunks):
        total = 0.0
        for c in chunks:
            span = pl.ds(tiles[c], tiles[c + 1] - tiles[c])
            total += jnp.dot(
                low_t[:, span], occ_far[span, :], preferred_element_type=jnp.float32
            )
        return total

    def buffers(r):
        cols = span_of(r)
        return part.at[:, cols], rs.at[:, :, cols], gyb.at[:, :, cols]

    def margins(r):
        sums, slots, _ = buffers(r)
        if r == last - 1:
            sums[...] += far_margins((1, 3))
        else:
            for i, at in enumerate(rounds[r]):
                sums[:, i * bands : (i + 1) * bands] = jnp.dot(
                    low_t[...], occ[at], preferred_element_type=jnp.float32
                )
        copies = spread(
            lambda p: sums.at[pl.ds(pl.multiple_of(p * share, 16), share)],
            lambda p: slots.at[my_z],
            (r, 0), "gz", my_z, nz,
        )
        slots[my_z] = sums[pl.ds(pl.multiple_of(my_z * share, 16), share), :]
        return copies

    def summed(slots, count):
        total = slots[0]
        for at in range(1, count):
            total += slots[at]
        return total

    def over_y(r, copies):
        arrive(copies)
        _, slots, shares = buffers(r)
        shares[my_y] = summed(slots, nz)
        return spread(
            lambda p: shares.at[my_y], lambda p: shares.at[my_y], (r, 1), "gy", my_y, ny
        )

    def over_z(r, copies):
        arrive(copies)
        cols = span_of(r)
        total = summed(buffers(r)[2], ny)
        mine = pl.ds(pl.multiple_of(my_z * share, 16), share)
        rows = coeff_far.at[mine] if r == last - 1 else coeff.at[mine, cols]
        rows[...] = (total / total_cells).astype(coeff.dtype)
        return spread(lambda p: rows, lambda p: rows, (r, 2), "gz", my_z, nz)

    def correct(r, copies):
        arrive(copies)

        def rows(y, carry):
            row = pl.ds(pl.multiple_of(y * flat, 16), flat)
            total = trial[row, :]
            for i, at in enumerate(rounds[r]):
                total -= lax.dot_general(
                    occ[at, row, :], coeff[:, pl.ds(starts[r] + i * bands, bands)],
                    (((1,), (1,)), ((), ())), preferred_element_type=jnp.float32,
                )
            trial[row, :] = total
            return carry

        lax.fori_loop(0, rows_y, rows, 0)

    def settle(copies):
        for copy in copies:
            copy.wait_send()

    flying = None
    for r in range(last):
        dist, final = r + 1, r == last - 1
        ending = None
        if r == last - 2 and flying is not None:
            ending = (flying[0], over_z(*flying))
            flying = None
        if final:
            advance(4 * r + 1)
            part[:, span_of(r)] = far_margins((0, 2))
        advance(4 * dist)
        one = margins(r)
        if r == 0:
            arrive(sq_copies)
            over = sq_z[0]
            for at in range(1, nz):
                over += sq_z[at]
            sq_y[my_y] = over
            sq_copies = spread(
                lambda p: sq_y.at[my_y], lambda p: sq_y.at[my_y], (last, 1), "gy", my_y, ny
            )
        if ending is not None:
            correct(*ending)
        if r < last - 2:
            advance(4 * dist + 1)
        two = over_y(r, one)
        if flying is not None:
            ending = (flying[0], over_z(*flying))
            if not final:
                advance(4 * dist + 2)
                correct(*ending)
        flying = (r, two)

    arrive(sq_copies)
    over = sq_y[0]
    for at in range(1, ny):
        over += sq_y[at]
    norm_ref[...] = jnp.sqrt(jnp.sum(over, axis=0, keepdims=True) / total_cells + 1e-06)

    settle(list(sends))
    three = over_z(*flying)
    if ending is not None:
        correct(*ending)
    arrive(three)
    settle(three)


def far_correction(trial, occ_far, coeff_far, norm_ref, out_hbm, norm_out, held, sems):
    rows_y, flat, bands = out_hbm.shape
    copies = [pltpu.make_async_copy(norm_ref, norm_out, sems.at[rows_y])]
    copies[0].start()
    for y in range(rows_y):
        row = pl.ds(y * flat, flat)
        held[row, :] = trial[row, :] - lax.dot_general(
            occ_far[row, :], coeff_far[...],
            (((1,), (1,)), ((), ())), preferred_element_type=jnp.float32,
        )
        copies.append(pltpu.make_async_copy(held.at[row], out_hbm.at[y], sems.at[y]))
        copies[-1].start()
    for copy in copies:
        copy.wait()


def on_device(nb, ny, nz, orbitals, occupied, eigen, potential, perturbation, precondition):
    bands, rows_y, flat = orbitals.shape
    cells = rows_y * flat
    padded = -(-cells // 128) * 128
    total_cells = float(cells * ny * nz)
    psi = jnp.transpose(orbitals, (1, 2, 0))
    occ = jnp.transpose(occupied, (1, 2, 0)).reshape(cells, bands)
    rounds = len(round_plan(nb))
    entries = len(ring_plan(nb)[0])
    share = bands // nz
    off_chip = pl.BlockSpec(memory_space=pltpu.HBM)
    local = pl.BlockSpec(memory_space=pltpu.VMEM)
    f32, bf16 = jnp.float32, jnp.bfloat16
    dma = pltpu.SemaphoreType.DMA
    held_bytes = padded * bands * 6 + bands * bands * 2 + 8192
    held = pl.pallas_call(
        functools.partial(kernel, nb, ny, nz, total_cells),
        out_shape=(
            pltpu.VMEM((padded, bands), f32),
            pltpu.VMEM((padded, bands), bf16),
            pltpu.VMEM((bands, bands), bf16),
            pltpu.VMEM((1, bands), f32),
        ),
        in_specs=[off_chip] * 6,
        out_specs=(local, local, local, local),
        scratch_shapes=[
            pltpu.VMEM((1, bands), f32),
            pltpu.VMEM((3, rows_y, flat), f32),
            pltpu.VMEM((rows_y + 2 * REACH, flat, bands), f32),
            pltpu.VMEM((rows_y, flat + 2 * REACH * NX, bands), f32),
            pltpu.VMEM((3, cells, bands), f32),
            pltpu.VMEM((nb, padded, bands), bf16),
            pltpu.VMEM((bands, padded), bf16),
            pltpu.VMEM((bands, nb * bands), f32),
            pltpu.VMEM((nz, share, nb * bands), f32),
            pltpu.VMEM((ny, share, nb * bands), f32),
            pltpu.VMEM((bands, nb * bands), bf16),
            pltpu.VMEM((nz, 8, bands), f32),
            pltpu.VMEM((ny, 8, bands), f32),
            dma((7,)), dma((4,)), dma((4,)), dma((2, entries)), dma((2, entries)),
            dma((rounds + 1, 3, max(ny, nz))), dma((rounds + 1, 3, max(ny, nz))),
            pltpu.SemaphoreType.REGULAR((2, max(max(ny, nz) // 2 - 1, 1), 2)),
        ],
        compiler_params=pltpu.CompilerParams(
            collective_id=0, has_side_effects=True, vmem_limit_bytes=67043328 - held_bytes
        ),
        name="sternheimer",
    )(psi, occ, eigen.reshape(1, bands), potential, perturbation, precondition)
    updated, norms = pl.pallas_call(
        far_correction,
        out_shape=(
            jax.ShapeDtypeStruct((rows_y, flat, bands), f32),
            jax.ShapeDtypeStruct((1, bands), f32),
        ),
        in_specs=[local] * 4,
        out_specs=(off_chip, off_chip),
        scratch_shapes=[pltpu.VMEM((cells, bands), f32), dma((rows_y + 1,))],
        compiler_params=pltpu.CompilerParams(vmem_limit_bytes=16 * 1024 * 1024),
        name="far_correction",
    )(*held)
    return jnp.transpose(updated, (2, 0, 1)), norms.reshape(bands)


def solution(mesh):
    placed = (
        P("band", "gy", "gz"),
        P("band", "gy", "gz"),
        P("band"),
        P("gy", "gz"),
        P("gy", "gz"),
        P("gy", "gz"),
    )
    sizes = tuple(mesh.shape[axis] for axis in ("band", "gy", "gz"))
    return jax.shard_map(
        functools.partial(on_device, *sizes),
        mesh=mesh,
        in_specs=placed,
        out_specs=(P("band", "gy", "gz"), P("band")),
        check_vma=False,
    )
```
